32 devices in a mesh: gx: 2 (over y), gy: 16 (over z, x, core).
Axes of the slice: x: 2, y: 2, z: 4, core: 2. Of those that a mesh axis runs over, the one named last changes fastest.
Arguments:
- state: float32 [5, 8, 1024, 768], P(None, None, 'gy', 'gx'), may hold values from -6 to 6
- driving: float32 [5, 8, 1024, 768], P(None, None, 'gy', 'gx'), may hold values from -6 to 6
- rate: float32 [5, 8], replicated, may hold values from 1 to 6
- sound_square: float32 [8, 1024, 768], P(None, 'gy', 'gx'), may hold values from 0.3 to 1
Outputs:
- nudged: float32 [5, 8, 1024, 768], P(None, None, 'gy', 'gx')
The draws below stay inside these ranges and needn't reach their ends.
All inputs are finite; a program needn't handle non-finite values.
Results may differ from the reference program's by a relative error of at most 0.000064.
Values sent between devices are 32-bit elements; how exact they have to be, the bound alone decides.
No kernel may reach another device: no remote copies, remote signals or barrier semaphores. Data moves between devices by JAX's collectives and lax.ppermute only.
A program may use at most 128 MiB of HBM per device.

```python
import math
import jax
import jax.numpy as jnp
from jax import lax

NFIELD = 5
MODES = 64
SUBSTEPS = 3
LEVELS = 8
NX = 768
NY = 1024


def block_scale(key, dims, cuts, low, high):
    def one(axis_at, shards_of):
        steps = jax.random.uniform(jax.random.fold_in(jax.random.fold_in(key, 6), axis_at), (shards_of,), jnp.float32, low / len(cuts), high / len(cuts))
        return jnp.repeat(jnp.exp(steps), dims[axis_at] // shards_of).reshape((-1,) + (1,) * (len(dims) - axis_at - 1))

    level = one(*cuts[0])
    for cut in cuts[1:]:
        level = level * one(*cut)
    return level


def centred(key, dims, scale, limit, cuts=(), held_as=jnp.bfloat16):
    gain = block_scale(key, dims, cuts, -0.22, 0.18) if cuts else 1.0
    array = jax.random.normal(key, dims, jnp.float32) * scale * gain
    return jnp.minimum(jnp.maximum(array, -limit), limit).astype(held_as)


def setup_inputs(seed: int = 0) -> dict:
    splits = jax.random.split(jax.random.key(seed), 5)
    return {
        "state": centred(splits[0], (NFIELD, LEVELS, NY, NX), 1.0, 6.0, ((2, 16), (3, 2)), jnp.float32),
        "driving": centred(splits[1], (NFIELD, LEVELS, NY, NX), 1.0, 6.0, ((2, 16), (3, 2)), jnp.float32),
        "rate": jnp.clip(jnp.exp(jax.random.uniform(splits[2], (NFIELD, LEVELS), jnp.float32, math.log(1.0), math.log(6.0))), 1.0, 6.0),
        "sound_square": jnp.clip(jnp.exp(math.log(1.0) - 1.2039728 * jax.random.uniform(splits[3], (LEVELS, NY, NX), jnp.float32) ** block_scale(splits[3], (LEVELS, NY, NX), ((1, 16), (2, 2)), -0.2, 0.2)), 0.3, 1.0),
    }


courant = 0.5


def tables(count, size):
    index = jnp.arange(size, dtype=jnp.int32)
    order = jnp.arange(count, dtype=jnp.int32)
    freq = jnp.where(order < count // 2, order, order - count // 2 + 1)
    wrapped = (freq[:, None] * (2 * index[None, :] + 1)) % (2 * size)
    phase = jnp.pi * wrapped.astype(jnp.float32) / size
    basis = jnp.where(order[:, None] < count // 2, jnp.cos(phase), jnp.sin(phase))
    scaling = jnp.where(order == 0, 1.0 / size, 2.0 / size).astype(jnp.float32)
    return basis, basis * scaling[:, None]


def vertical(field):
    padded = jnp.pad(field, ((1, 1), (0, 0), (0, 0)))
    return 0.5 * (padded[2:] - padded[:-2])


def horizontal(field):
    padded = jnp.pad(field, ((0, 0), (1, 1), (1, 1)))
    across = 0.5 * (padded[:, 1:-1, 2:] - padded[:, 1:-1, :-2])
    along = 0.5 * (padded[:, 2:, 1:-1] - padded[:, :-2, 1:-1])
    return across, along


def substep(fields, sound_square):
    wind_u, wind_v, wind_w, press, theta = fields
    press_x, press_y = horizontal(press)
    new_u = wind_u - courant * press_x
    new_v = wind_v - courant * press_y
    new_w = wind_w - courant * vertical(press) + courant * theta
    u_x, _ = horizontal(new_u)
    _, v_y = horizontal(new_v)
    diverge = u_x + v_y + vertical(new_w)
    new_p = press - courant * sound_square * diverge
    new_t = theta - courant * new_w
    return (new_u, new_v, new_w, new_p, new_t)


def reference(state, driving, rate, sound_square):
    high = lax.Precision.HIGHEST
    basis_x, weight_x = tables(MODES, NX)
    basis_y, weight_y = tables(MODES, NY)
    difference = state - driving
    partial_value = jnp.einsum('flyx,kx->flyk', difference, weight_x, precision=high)
    modes = jnp.einsum('flyk,jy->fljk', partial_value, weight_y, precision=high)
    scaled = rate[:, :, None, None] * modes
    rows_back = jnp.einsum('fljk,jy->flyk', scaled, basis_y, precision=high)
    tendency = jnp.einsum('flyk,kx->flyx', rows_back, basis_x, precision=high)
    fields = tuple(state[i] for i in range(NFIELD))
    for step in range(SUBSTEPS):
        fields = substep(fields, sound_square)
    advanced = jnp.stack(fields)
    return advanced - tendency
```

```python
import functools

import jax
import jax.numpy as jnp
import numpy as np
from jax import lax
from jax.experimental import pallas as pl
from jax.experimental.pallas import tpu as pltpu
from jax.sharding import PartitionSpec as P

MODES = 64
SUBSTEPS = 3
COURANT = 0.5
LANES = 128
SUB = 8
GUARD = 8

REACH_X = (5, 4, 4, 6, 4, 4)
GROUP_X = (0, 0, 1, 0, 1, 1)


def lane_starts(levels):
    used = [0, 0]
    starts = []
    for width, group in zip(REACH_X, GROUP_X):
        starts.append(used[group])
        used[group] += width * levels
    assert max(used) <= LANES
    return starts


def bases(count, total):
    index = np.arange(total, dtype=np.int64)
    order = np.arange(count, dtype=np.int64)
    freq = np.where(order < count // 2, order, order - count // 2 + 1)
    wrapped = (freq[:, None] * (2 * index[None, :] + 1)) % (2 * total)
    phase = np.pi * wrapped.astype(np.float64) / total
    basis = np.where(order[:, None] < count // 2, np.cos(phase), np.sin(phase))
    scaling = np.where(order == 0, 1.0 / total, 2.0 / total)
    basis32 = basis.astype(np.float32)
    weight32 = (basis * scaling[:, None]).astype(np.float32)
    return basis32, weight32


def halves(table):
    high = table.astype(jnp.bfloat16)
    low = (table - high.astype(np.float32)).astype(jnp.bfloat16)
    return np.asarray(high), np.asarray(low)


def split(value):
    high = value.astype(jnp.bfloat16)
    low = (value - high.astype(jnp.float32)).astype(jnp.bfloat16)
    return high, low


def dot(left, right):
    return jnp.dot(left, right, preferred_element_type=jnp.float32)


def masks_of(bits):
    masks = [0]
    for bit in bits:
        masks = masks + [mask | (1 << bit) for mask in masks]
    return masks


def stages_of(devices):
    total = devices.bit_length() - 1
    assert devices == 1 << total
    left = list(range(total))
    stages = []
    if left:
        stages.append([left.pop(0)])
    while len(left) > 3 and len(stages) < 3:
        stages.append([left.pop(0), left.pop()])
    return stages, left


def pack_kernel(info, xs_ref, ss_ref, ya_ref, sya_ref, yb_ref, syb_ref, xo_ref, ao_ref, bo_ref, *, levels):
    right = info[3]
    lane = lax.broadcasted_iota(jnp.int32, (xo_ref.shape[0], LANES), 1)
    starts = lane_starts(levels)
    packed = [jnp.zeros((xo_ref.shape[0], LANES), jnp.float32) for _ in range(2)]
    for item in range(6):
        width, group = REACH_X[item], GROUP_X[item]
        for level in range(levels):
            tile = xs_ref[item, level] if item < 5 else ss_ref[level]
            first = starts[item] + width * level
            moved = pltpu.roll(tile, lax.rem(first + right * width, LANES), 1)
            packed[group] = jnp.where((lane >= first) & (lane < first + width), moved, packed[group])
    xo_ref[:, :LANES] = packed[0]
    xo_ref[:, LANES:] = packed[1]
    rows = lax.broadcasted_iota(jnp.int32, (SUB, ya_ref.shape[3]), 0)
    for bottom, src, sound, out in ((info[4], ya_ref, sya_ref, ao_ref), (1 - info[4], yb_ref, syb_ref, bo_ref)):
        own = (rows // 4) == bottom
        for level in range(levels):
            out[level, 0] = src[3, level]
            out[level, 1] = src[1, level]
            out[level, 2] = jnp.where(own, src[0, level], pltpu.roll(src[2, level], 4, 0))
            out[level, 3] = jnp.where(own, src[4, level], pltpu.roll(sound[level], 4, 0))


def project_kernel(info, state_ref, driving_ref, wx_ref, wy_ref, keep_ref, send_ref, modes_ref):
    levels, rows, cols = state_ref.shape[1:]
    half = levels // 2
    pieces = 2 * keep_ref.shape[0]
    chunk = keep_ref.shape[2]
    lane = lax.broadcasted_iota(jnp.int32, (half * rows, LANES), 1)
    weights = wx_ref[0]
    sides = []
    for side in range(2):
        part = pl.ds(side * half, half)
        diff = (state_ref[0, part] - driving_ref[0, part]).reshape(half * rows, cols)
        high, low = split(diff)
        both = dot(high, weights) + dot(low, weights)
        sides.append(both + pltpu.roll(both, MODES, 1))
    packed = jnp.where(lane < MODES, sides[0], sides[1])
    high, low = split(packed)
    stacked = jnp.concatenate([high, low], axis=1)
    for pair in range(half):
        out = dot(wy_ref[0], stacked[pair * rows : (pair + 1) * rows])
        out = out[:MODES] + out[MODES:]
        modes_ref[pair * MODES : (pair + 1) * MODES] = out[:, :LANES] + out[:, LANES:]
    mine = info[2]
    for piece in range(pieces):
        source = pl.multiple_of(jnp.bitwise_xor(mine, piece) * chunk, SUB)
        target = keep_ref if piece < pieces // 2 else send_ref
        target[piece % (pieces // 2), 0] = modes_ref[pl.ds(source, chunk)]


def final_kernel(info, rate_ref, adv_ref, own_ref, far_ref, bx_ref, by_ref, out_ref, modes_ref, wide_ref):
    levels, rows, cols = adv_ref.shape[1:]
    half = levels // 2
    pieces = 2 * own_ref.shape[0]
    chunk = own_ref.shape[2]
    field = pl.program_id(0)

    @pl.when(field == 0)
    def _():
        wide_ref[...] = jnp.zeros_like(wide_ref)
        for copy in range(3):
            piece = bx_ref[0, copy // 2]
            wide_ref[copy * 2 * MODES : copy * 2 * MODES + MODES, :cols] = piece
            wide_ref[copy * 2 * MODES + MODES : (copy + 1) * 2 * MODES, cols:] = piece

    mine = info[2]
    for piece in range(pieces):
        target = pl.multiple_of(jnp.bitwise_xor(mine, piece) * chunk, SUB)
        source = own_ref if piece < pieces // 2 else far_ref
        modes_ref[pl.ds(target, chunk)] = source[piece % (pieces // 2), 0]
    lane = lax.broadcasted_iota(jnp.int32, (MODES, LANES), 1)
    backs = []
    for pair in range(half):
        factor = jnp.where(lane < MODES, rate_ref[field, pair], rate_ref[field, pair + half])
        high, low = split(modes_ref[pair * MODES : (pair + 1) * MODES] * factor)
        out = dot(by_ref[0], jnp.concatenate([high, low], axis=1))
        out = out[:rows] + out[rows:]
        backs.append(out[:, :LANES] + out[:, LANES:])
    high, low = split(jnp.concatenate(backs, axis=0))
    left = jnp.concatenate([high, low], axis=1)
    tendency = dot(left, wide_ref[: 4 * MODES]) + dot(high, wide_ref[4 * MODES :])
    for side in range(2):
        part = pl.ds(side * half, half)
        piece = tendency[:, side * cols : (side + 1) * cols].reshape(half, rows, cols)
        out_ref[0, part] = adv_ref[0, part] - piece


def stencil_kernel(info, *refs, x_phases, levels, rows, cols):
    state_ref, sound_ref = refs[:2]
    bands = refs[2 : 2 + x_phases]
    slabs = refs[2 + x_phases : 4 + x_phases]
    corners = refs[4 + x_phases : 6 + x_phases]
    out_ref = refs[6 + x_phases]
    ext = refs[7 + x_phases : 13 + x_phases]
    in_sem, out_sem = refs[13 + x_phases :]
    tiles = cols // LANES
    chunks = rows // SUB
    main = GUARD + SUB

    def load(item):
        copies = []
        for tile in range(tiles):
            src = state_ref.at[item] if item < 5 else sound_ref
            copies.append(
                pltpu.make_async_copy(
                    src.at[:, :, pl.ds(tile * LANES, LANES)],
                    ext[item].at[:, tile, pl.ds(main, rows)],
                    in_sem.at[item, tile],
                )
            )
        return copies

    loads = [load(item) for item in range(6)]
    for item in (3, 0, 1, 2, 4, 5):
        for copy in loads[item]:
            copy.start()

    starts = lane_starts(levels)
    lane = lax.broadcasted_iota(jnp.int32, (SUB, LANES), 1)
    odd_x, odd_y = info[5], info[6]

    def halo_lanes(sources, item, level):
        width, group = REACH_X[item], GROUP_X[item]
        first = starts[item] + width * level
        value = jnp.zeros((SUB, LANES), jnp.float32)
        for phase, source in enumerate(sources):
            left = odd_x if phase == 0 else 1 - odd_x
            moved = pltpu.roll(source(group), lax.rem(2 * LANES - first - left * width, LANES), 1)
            from_edge = jnp.where(left == 1, LANES - 1 - lane, lane)
            value = jnp.where(from_edge < width, moved, value)
        return value

    zero = jnp.zeros((SUB, LANES), jnp.float32)
    for item in range(6):
        for level in range(levels):
            for tile in range(tiles + 1):
                if item in (1, 3):
                    ext[item][level, tile, pl.ds(0, SUB)] = zero
                    ext[item][level, tile, pl.ds(main + rows + SUB, SUB)] = zero

    def band_rows(chunk, _):
        row = pl.multiple_of(chunk * SUB, SUB)
        for item in range(6):
            for level in range(levels):
                sources = [
                    (lambda group, band=band: band[pl.ds(row, SUB), group * LANES : (group + 1) * LANES])
                    for band in bands
                ]
                ext[item][level, tiles, pl.ds(row + main, SUB)] = halo_lanes(sources, item, level)
        return 0

    lax.fori_loop(0, chunks, band_rows, 0)

    order = ((3, 0, None), (1, 1, None), (0, 2, 0), (2, 2, 4), (4, 3, 0), (5, 3, 4))
    for phase in range(2):
        top = odd_y if phase == 0 else 1 - odd_y
        base = pl.multiple_of(jnp.where(top == 1, GUARD, main + rows), SUB)
        for item, place, turn in order:
            for level in range(levels):
                for tile in range(tiles):
                    value = slabs[phase][level, place, :, tile * LANES : (tile + 1) * LANES]
                    if turn == 4:
                        value = pltpu.roll(value, 4, 0)
                    ext[item][level, tile, pl.ds(base, SUB)] = value
                sources = [
                    (
                        lambda group, index=index: corners[phase][
                            :, (2 * index + group) * LANES : (2 * index + group + 1) * LANES
                        ]
                    )
                    for index in range(x_phases)
                ]
                ext[item][level, tiles, pl.ds(base, SUB)] = halo_lanes(sources, item, level)

    quarter = 0.5 * COURANT
    has_left, has_right = info[7], info[8]
    has_top, has_bottom = info[9], info[10]
    edge = jnp.where(
        lane < LANES // 2,
        jnp.where(has_right == 1, quarter, 0.0),
        jnp.where(has_left == 1, quarter, 0.0),
    )
    first_lane, last_lane = lane == 0, lane == LANES - 1

    def across(values, tile):
        count = tiles + 1
        ahead = jnp.where(first_lane, values[(tile + 1) % count], values[tile])
        behind = jnp.where(last_lane, values[(tile - 1) % count], values[tile])
        return pltpu.roll(ahead, LANES - 1, 1) - pltpu.roll(behind, 1, 1)

    u_ref, v_ref, w_ref, p_ref, t_ref, s_ref = ext

    def winds(chunk, row, x_tiles, only_v):
        here = pl.ds(row, SUB)
        rise = jnp.where(chunk == 0, jnp.where(has_top == 1, quarter, 0.0), quarter)
        rise = jnp.where(chunk == chunks + 1, jnp.where(has_bottom == 1, quarter, 0.0), rise)
        for tile in range(x_tiles):
            for level in range(levels):
                step = p_ref[level, tile, pl.ds(row + 1, SUB)] - p_ref[level, tile, pl.ds(row - 1, SUB)]
                v_ref[level, tile, here] = v_ref[level, tile, here] - rise * step
        if only_v:
            return
        for level in range(levels):
            line = [p_ref[level, tile, here] for tile in range(tiles + 1)]
            for tile in range(tiles + 1):
                factor = quarter if tile < tiles else edge
                u_ref[level, tile, here] = u_ref[level, tile, here] - factor * across(line, tile)
        for tile in range(x_tiles):
            for level in range(levels):
                if level == 0:
                    lift = p_ref[1, tile, here]
                elif level == levels - 1:
                    lift = -p_ref[level - 1, tile, here]
                else:
                    lift = p_ref[level + 1, tile, here] - p_ref[level - 1, tile, here]
                w_ref[level, tile, here] = (
                    w_ref[level, tile, here] - quarter * lift + COURANT * t_ref[level, tile, here]
                )

    def scalars(row, x_tiles):
        here = pl.ds(row, SUB)
        for level in range(levels):
            line = [u_ref[level, tile, here] for tile in range(tiles + 1)]
            for tile in range(x_tiles):
                spread = across(line, tile)
                spread += v_ref[level, tile, pl.ds(row + 1, SUB)] - v_ref[level, tile, pl.ds(row - 1, SUB)]
                if level == 0:
                    spread += w_ref[1, tile, here]
                elif level == levels - 1:
                    spread -= w_ref[level - 1, tile, here]
                else:
                    spread += w_ref[level + 1, tile, here] - w_ref[level - 1, tile, here]
                p_ref[level, tile, here] = (
                    p_ref[level, tile, here] - (quarter * s_ref[level, tile, here]) * spread
                )
                t_ref[level, tile, here] = t_ref[level, tile, here] - COURANT * w_ref[level, tile, here]

    for item in (3, 0, 1, 2, 4, 5):
        for copy in loads[item]:
            copy.wait()

    def store(item):
        copies = []
        for tile in range(tiles):
            copies.append(
                pltpu.make_async_copy(
                    ext[item].at[:, tile, pl.ds(main, rows)],
                    out_ref.at[item, :, :, pl.ds(tile * LANES, LANES)],
                    out_sem.at[item, tile],
                )
            )
        return copies

    stores = [store(item) for item in range(5)]
    for step in range(SUBSTEPS):
        last = step == SUBSTEPS - 1
        x_tiles = tiles if last else tiles + 1
        low, count = (1, chunks) if last else (0, chunks + 2)

        def wind_rows(chunk, _, x_tiles=x_tiles):
            winds(chunk, pl.multiple_of(GUARD + chunk * SUB, SUB), x_tiles, False)
            return 0

        def scalar_rows(chunk, _, x_tiles=x_tiles):
            scalars(pl.multiple_of(GUARD + chunk * SUB, SUB), x_tiles)
            return 0

        if last:
            winds(0, GUARD, x_tiles, True)
            winds(chunks + 1, GUARD + (chunks + 1) * SUB, x_tiles, True)
        lax.fori_loop(low, low + count, wind_rows, 0)
        if last:
            for item in (0, 1, 2):
                for copy in stores[item]:
                    copy.start()
        lax.fori_loop(low, low + count, scalar_rows, 0)
    for item in (3, 4):
        for copy in stores[item]:
            copy.start()
    for item in range(5):
        for copy in stores[item]:
            copy.wait()


def solution(mesh):
    nx, ny = mesh.shape["gx"], mesh.shape["gy"]
    devices = nx * ny
    stages, middle = stages_of(devices)
    pieces = 1
    for stage in stages:
        pieces *= 1 << len(stage)
    pieces = max(pieces, 2)

    numbers = np.arange(devices)
    mine = np.zeros(devices, np.int64)
    for stage in stages:
        digit = np.zeros(devices, np.int64)
        for place, bit in enumerate(stage):
            digit |= ((numbers >> bit) & 1) << place
        mine = (mine << len(stage)) | digit
    gx, gy = numbers // ny, numbers % ny
    info_table = np.stack(
        [
            gx,
            gy,
            mine,
            (gx + 1) % 2,
            (gy + 1) % 2,
            gx % 2,
            gy % 2,
            gx > 0,
            gx < nx - 1,
            gy > 0,
            gy < ny - 1,
            gx * 0,
        ],
        axis=1,
    ).astype(np.int32)

    x_phases = 1 if nx == 2 else 2

    def swap(value, mask):
        return lax.ppermute(value, ("gx", "gy"), [(i, i ^ mask) for i in range(devices)])

    def neighbours(value, axis, count, phase):
        pairs = []
        for low in range(phase, count - 1, 2):
            pairs += [(low, low + 1), (low + 1, low)]
        return lax.ppermute(value, axis, pairs)

    def on_device(state, driving, rate, sound_square):
        fields, levels, rows, cols = state.shape
        half = levels // 2
        chunk = half * MODES // pieces
        number = lax.axis_index("gx") * ny + lax.axis_index("gy")
        info = lax.dynamic_slice(jnp.asarray(info_table), (number, 0), (1, info_table.shape[1]))[0]
        other = None
        if x_phases == 2:
            flip = np.zeros(info_table.shape[1], np.int32)
            flip[3] = 1
            other = jnp.abs(jnp.asarray(flip) - info)

        basis_x, weight_x = bases(MODES, cols * nx)
        basis_y, weight_y = bases(MODES, rows * ny)
        high, low = halves(weight_x)
        wx = np.concatenate([high, low], axis=0).T.reshape(nx, cols, 2 * MODES)
        high, low = halves(weight_y)
        wy = np.concatenate([high, low], axis=0).reshape(2 * MODES, ny, rows).transpose(1, 0, 2)
        high, low = halves(basis_x)
        bx = np.stack([high, low]).reshape(2, MODES, nx, cols).transpose(2, 0, 1, 3)
        high, low = halves(basis_y)
        by = np.stack([high, low]).reshape(2, MODES, ny, rows).transpose(2, 0, 3, 1).reshape(ny, 2 * rows, MODES)
        wx, wy, bx, by = (jnp.asarray(np.ascontiguousarray(t)) for t in (wx, wy, bx, by))

        last_tile, last_rows = cols // LANES - 1, rows // SUB - 1

        def pack(info):
            return pl.pallas_call(
                functools.partial(pack_kernel, levels=levels),
                grid_spec=pltpu.PrefetchScalarGridSpec(
                    num_scalar_prefetch=1,
                    grid=(1,),
                    in_specs=[
                        pl.BlockSpec((fields, levels, rows, LANES), lambda i, s: (0, 0, 0, s[3] * last_tile)),
                        pl.BlockSpec((levels, rows, LANES), lambda i, s: (0, 0, s[3] * last_tile)),
                        pl.BlockSpec((fields, levels, SUB, cols), lambda i, s: (0, 0, s[4] * last_rows, 0)),
                        pl.BlockSpec((levels, SUB, cols), lambda i, s: (0, s[4] * last_rows, 0)),
                        pl.BlockSpec((fields, levels, SUB, cols), lambda i, s: (0, 0, (1 - s[4]) * last_rows, 0)),
                        pl.BlockSpec((levels, SUB, cols), lambda i, s: (0, (1 - s[4]) * last_rows, 0)),
                    ],
                    out_specs=[
                        pl.BlockSpec((rows, 2 * LANES), lambda i, s: (0, 0)),
                        pl.BlockSpec((levels, 4, SUB, cols), lambda i, s: (0, 0, 0, 0)),
                        pl.BlockSpec((levels, 4, SUB, cols), lambda i, s: (0, 0, 0, 0)),
                    ],
                ),
                out_shape=[
                    jax.ShapeDtypeStruct((rows, 2 * LANES), jnp.float32),
                    jax.ShapeDtypeStruct((levels, 4, SUB, cols), jnp.float32),
                    jax.ShapeDtypeStruct((levels, 4, SUB, cols), jnp.float32),
                ],
                name="pack",
            )(info, state, sound_square, state, sound_square, state, sound_square)

        band, slab_a, slab_b = pack(info)
        bands = [neighbours(band, "gx", nx, 0)]
        if x_phases == 2:
            bands.append(neighbours(pack(other)[0], "gx", nx, 1))
        slabs = [neighbours(slab_a, "gy", ny, 0), neighbours(slab_b, "gy", ny, 1)]
        joined = jnp.concatenate(bands, axis=1) if len(bands) > 1 else bands[0]
        head, tail = joined[:SUB], joined[rows - SUB :]
        to_tail = info[4] == 1
        corners = [
            neighbours(jnp.where(to_tail, tail, head), "gy", ny, 0),
            neighbours(jnp.where(to_tail, head, tail), "gy", ny, 1),
        ]

        piece_shape = (pieces // 2, fields, chunk, LANES)
        keep, send = pl.pallas_call(
            project_kernel,
            grid_spec=pltpu.PrefetchScalarGridSpec(
                num_scalar_prefetch=1,
                grid=(fields,),
                in_specs=[
                    pl.BlockSpec((1, levels, rows, cols), lambda f, s: (f, 0, 0, 0)),
                    pl.BlockSpec((1, levels, rows, cols), lambda f, s: (f, 0, 0, 0)),
                    pl.BlockSpec((1, cols, 2 * MODES), lambda f, s: (s[0], 0, 0)),
                    pl.BlockSpec((1, 2 * MODES, rows), lambda f, s: (s[1], 0, 0)),
                ],
                out_specs=[
                    pl.BlockSpec((pieces // 2, 1, chunk, LANES), lambda f, s: (0, f, 0, 0)),
                    pl.BlockSpec((pieces // 2, 1, chunk, LANES), lambda f, s: (0, f, 0, 0)),
                ],
                scratch_shapes=[pltpu.VMEM((half * MODES, LANES), jnp.float32)],
            ),
            out_shape=[jax.ShapeDtypeStruct(piece_shape, jnp.float32)] * 2,
            cost_estimate=pl.CostEstimate(flops=600_000_000, bytes_accessed=8_500_000, transcendentals=0),
            name="project",
        )(info, state, driving, wx, wy)

        value = None
        for place, stage in enumerate(stages):
            masks = masks_of(stage)
            if place == 0:
                value = keep + swap(send, masks[1])
                continue
            value = value.reshape((len(masks), value.shape[0] // len(masks)) + value.shape[1:])
            moved = [swap(value[i], masks[i]) for i in range(1, len(masks))]
            value = functools.reduce(jnp.add, moved, value[0])
        moved = [swap(value, mask) for mask in masks_of(middle)[1:]]
        value = functools.reduce(jnp.add, moved, value)
        for stage in reversed(stages[1:]):
            masks = masks_of(stage)
            value = jnp.concatenate([value] + [swap(value, mask) for mask in masks[1:]], axis=0)
        far = swap(value, masks_of(stages[0])[1])

        any_space = pl.BlockSpec(memory_space=pl.ANY)
        in_vmem = pl.BlockSpec(memory_space=pltpu.VMEM)
        tiles = cols // LANES
        advanced = pl.pallas_call(
            functools.partial(stencil_kernel, x_phases=x_phases, levels=levels, rows=rows, cols=cols),
            grid_spec=pltpu.PrefetchScalarGridSpec(
                num_scalar_prefetch=1,
                grid=(1,),
                in_specs=[any_space, any_space] + [in_vmem] * (x_phases + 4),
                out_specs=any_space,
                scratch_shapes=[
                    pltpu.VMEM((levels, tiles + 1, rows + 2 * SUB + 2 * GUARD, LANES), jnp.float32)
                    for _ in range(6)
                ]
                + [pltpu.SemaphoreType.DMA((6, tiles)), pltpu.SemaphoreType.DMA((5, tiles))],
            ),
            out_shape=jax.ShapeDtypeStruct(state.shape, jnp.float32),
            cost_estimate=pl.CostEstimate(flops=30_000_000, bytes_accessed=20_000_000, transcendentals=0),
            name="substeps",
        )(info, state, sound_square, *bands, *slabs, *corners)

        return pl.pallas_call(
            final_kernel,
            grid_spec=pltpu.PrefetchScalarGridSpec(
                num_scalar_prefetch=2,
                grid=(fields,),
                in_specs=[
                    pl.BlockSpec((1, levels, rows, cols), lambda f, s, r: (f, 0, 0, 0)),
                    pl.BlockSpec((pieces // 2, 1, chunk, LANES), lambda f, s, r: (0, f, 0, 0)),
                    pl.BlockSpec((pieces // 2, 1, chunk, LANES), lambda f, s, r: (0, f, 0, 0)),
                    pl.BlockSpec((1, 2, MODES, cols), lambda f, s, r: (s[0], 0, 0, 0)),
                    pl.BlockSpec((1, 2 * rows, MODES), lambda f, s, r: (s[1], 0, 0)),
                ],
                out_specs=pl.BlockSpec((1, levels, rows, cols), lambda f, s, r: (f, 0, 0, 0)),
                scratch_shapes=[
                    pltpu.VMEM((half * MODES, LANES), jnp.float32),
                    pltpu.VMEM((6 * MODES, 2 * cols), jnp.bfloat16),
                ],
            ),
            out_shape=jax.ShapeDtypeStruct(state.shape, jnp.float32),
            cost_estimate=pl.CostEstimate(flops=600_000_000, bytes_accessed=8_500_000, transcendentals=0),
            name="nudge",
        )(info, rate, advanced, value, far, bx, by)

    return jax.shard_map(
        on_device,
        mesh=mesh,
        in_specs=(P(None, None, "gy", "gx"), P(None, None, "gy", "gx"), P(), P(None, "gy", "gx")),
        out_specs=P(None, None, "gy", "gx"),
        check_vma=False,
    )
```

```python
import functools

import jax
import jax.numpy as jnp
import numpy as np
from jax import lax
from jax.experimental import pallas as pl
from jax.experimental.pallas import tpu as pltpu
from jax.sharding import PartitionSpec as P


MODES = 64
SUBSTEPS = 3
COURANT = 0.5
LANES = 128
SUB = 8
GUARD = 8
VMEM_LIMIT = 32 << 20

REACH_X = (5, 4, 4, 6, 4, 4)
GROUP_X = (0, 0, 1, 0, 1, 1)


def lane_starts(levels):
    used = [0, 0]
    starts = []
    for width, group in zip(REACH_X, GROUP_X):
        starts.append(used[group])
        used[group] += width * levels
    assert max(used) <= LANES
    return starts


def bases(count, total):
    index = np.arange(total, dtype=np.int64)
    order = np.arange(count, dtype=np.int64)
    freq = np.where(order < count // 2, order, order - count // 2 + 1)
    wrapped = (freq[:, None] * (2 * index[None, :] + 1)) % (2 * total)
    phase = np.pi * wrapped.astype(np.float64) / total
    basis = np.where(order[:, None] < count // 2, np.cos(phase), np.sin(phase))
    scaling = np.where(order == 0, 1.0 / total, 2.0 / total)
    basis32 = basis.astype(np.float32)
    weight32 = (basis * scaling[:, None]).astype(np.float32)
    return basis32, weight32


def halves(table):
    high = table.astype(jnp.bfloat16)
    low = (table - high.astype(np.float32)).astype(jnp.bfloat16)
    return np.asarray(high), np.asarray(low)


def split(value):
    high = value.astype(jnp.bfloat16)
    low = (value - high.astype(jnp.float32)).astype(jnp.bfloat16)
    return high, low


def dot(left, right):
    return jnp.dot(left, right, preferred_element_type=jnp.float32)


def masks_of(bits):
    masks = [0]
    for bit in bits:
        masks = masks + [mask | (1 << bit) for mask in masks]
    return masks


def stages_of(devices):
    total = devices.bit_length() - 1
    assert devices == 1 << total
    left = list(range(total))
    stages = []
    if left:
        stages.append([left.pop(0)])
    while len(left) > 3 and len(stages) < 3:
        stages.append([left.pop(0), left.pop()])
    return stages, left


def slab_kernel(facts, state_ref, sound_ref, a_ref, b_ref, extra_ref, sem):
    levels, _, _, cols = a_ref.shape
    rows = state_ref.shape[2]
    bottom = facts[4]
    copies = []
    for phase, out_ref in enumerate((a_ref, b_ref)):
        last = bottom if phase == 0 else 1 - bottom
        here = pl.ds(pl.multiple_of(last * (rows - SUB), SUB), SUB)
        for place, (source, target) in enumerate(
            (
                (state_ref.at[3], out_ref.at[:, 0]),
                (state_ref.at[1], out_ref.at[:, 1]),
                (state_ref.at[0], out_ref.at[:, 2]),
                (state_ref.at[4], out_ref.at[:, 3]),
                (state_ref.at[2], extra_ref.at[phase, 0]),
                (sound_ref, extra_ref.at[phase, 1]),
            )
        ):
            copies.append(pltpu.make_async_copy(source.at[:, here], target, sem.at[phase, place]))
    for copy in copies:
        copy.start()
    for copy in copies:
        copy.wait()
    index = lax.broadcasted_iota(jnp.int32, (SUB, cols), 0)
    for phase, out_ref in enumerate((a_ref, b_ref)):
        last = bottom if phase == 0 else 1 - bottom
        own = (index // 4) == last
        for level in range(levels):
            for place in range(2):
                turned = pltpu.roll(extra_ref[phase, place, level], 4, 0)
                out_ref[level, 2 + place] = jnp.where(own, out_ref[level, 2 + place], turned)


def project_kernel(
    facts, state_ref, driving_ref, wx_hbm, wy_hbm, keep_ref, send_ref, held, other, wx_ref, wy_ref, packed_ref, modes_ref, sem
):
    fields, levels, rows, cols = state_ref.shape
    half = levels // 2
    pieces = 2 * keep_ref.shape[0]
    chunk = keep_ref.shape[2]
    tables = [
        pltpu.make_async_copy(wx_hbm.at[facts[0]], wx_ref, sem.at[fields, 0]),
        pltpu.make_async_copy(wy_hbm.at[facts[1]], wy_ref, sem.at[fields, 1]),
    ]
    loads = [
        [
            pltpu.make_async_copy(state_ref.at[field], held.at[field], sem.at[field, 0]),
            pltpu.make_async_copy(driving_ref.at[field], other.at[field], sem.at[field, 1]),
        ]
        for field in range(fields)
    ]
    for copy in [*loads[0], *tables, *(copy for load in loads[1:] for copy in load)]:
        copy.start()
    lane = lax.broadcasted_iota(jnp.int32, (half * rows, LANES), 1)
    for copy in tables:
        copy.wait()
    weights = wx_ref[...]
    for field in range(fields):
        for copy in loads[field]:
            copy.wait()
        sides = []
        for side in range(2):
            part = pl.ds(side * half, half)
            diff = (held[field, part] - other[field, part]).reshape(half * rows, cols)
            high, low = split(diff)
            both = dot(high, weights) + dot(low, weights)
            sides.append(both + pltpu.roll(both, MODES, 1))
        high, low = split(jnp.where(lane < MODES, sides[0], sides[1]))
        packed_ref[field, :, :LANES] = high
        packed_ref[field, :, LANES:] = low
    for field in range(fields):
        for pair in range(half):
            out = dot(wy_ref[...], packed_ref[field, pair * rows : (pair + 1) * rows])
            out = out[:MODES] + out[MODES:]
            modes_ref[field, pair * MODES : (pair + 1) * MODES] = out[:, :LANES] + out[:, LANES:]
    mine = facts[2]
    for piece in range(pieces):
        source = pl.multiple_of(jnp.bitwise_xor(mine, piece) * chunk, SUB)
        target = keep_ref if piece < pieces // 2 else send_ref
        target[piece % (pieces // 2)] = modes_ref[:, pl.ds(source, chunk)]


def nudge_kernel(facts, rate_ref, ext_ref, own_ref, far_ref, wide_ref, by_ref, out_ref, modes_ref, back_ref, done_ref, sem):
    fields, levels, rows, cols = out_ref.shape
    tiles = cols // LANES
    half = levels // 2
    pieces = 2 * own_ref.shape[0]
    chunk = own_ref.shape[2]
    mine = facts[2]
    for piece in range(pieces):
        target = pl.multiple_of(jnp.bitwise_xor(mine, piece) * chunk, SUB)
        source = own_ref if piece < pieces // 2 else far_ref
        modes_ref[:, pl.ds(target, chunk)] = source[piece % (pieces // 2)]
    lane = lax.broadcasted_iota(jnp.int32, (MODES, LANES), 1)
    for field in range(fields):
        for pair in range(half):
            factor = jnp.where(lane < MODES, rate_ref[field, pair], rate_ref[field, pair + half])
            high, low = split(modes_ref[field, pair * MODES : (pair + 1) * MODES] * factor)
            out = dot(by_ref[...], jnp.concatenate([high, low], axis=1))
            out = out[:rows] + out[rows:]
            high, low = split(out[:, :LANES] + out[:, LANES:])
            back_ref[field, pair * rows : (pair + 1) * rows, :LANES] = high
            back_ref[field, pair * rows : (pair + 1) * rows, LANES:] = low
    main = pl.ds(GUARD + SUB, rows)
    stores = []
    for field in range(fields):
        left = back_ref[field]
        tendency = dot(left, wide_ref[: 4 * MODES]) + dot(left[:, :LANES], wide_ref[4 * MODES :])
        for level in range(levels):
            first = (level % half) * rows
            for tile in range(tiles):
                lanes = pl.ds(tile * LANES, LANES)
                column = (level // half) * cols + tile * LANES
                done_ref[field, level, :, lanes] = (
                    ext_ref[field, level, tile, main] - tendency[first : first + rows, column : column + LANES]
                )
        stores.append(pltpu.make_async_copy(done_ref.at[field], out_ref.at[field], sem.at[field]))
        stores[-1].start()
    for copy in stores:
        copy.wait()


def band_lanes(level_count):
    starts = lane_starts(level_count)
    for item in range(6):
        for level in range(level_count):
            yield item, level, REACH_X[item], GROUP_X[item], starts[item] + REACH_X[item] * level


def load_kernel(facts, state_ref, sound_ref, a_ref, b_ref, bx_hbm, by_hbm, ext_ref, wide_ref, by_ref, *refs):
    *bands, sem = refs
    _, levels, rows, cols = state_ref.shape
    tiles = cols // LANES
    main = GUARD + SUB
    loads = []
    for tile in dict.fromkeys((0, tiles - 1, *range(tiles))):
        for item in range(6):
            source = state_ref.at[item] if item < 5 else sound_ref
            loads.append(
                pltpu.make_async_copy(
                    source.at[:, :, pl.ds(tile * LANES, LANES)],
                    ext_ref.at[item, :, tile, pl.ds(main, rows)],
                    sem.at[item, tile],
                )
            )
    tables = [pltpu.make_async_copy(by_hbm.at[facts[1]], by_ref, sem.at[6, 0])]
    for copy in range(3):
        for side in range(2):
            target = wide_ref.at[
                pl.ds((2 * copy + side) * MODES, MODES), pl.ds(side * cols, cols)
            ]
            tables.append(pltpu.make_async_copy(bx_hbm.at[facts[0], copy // 2], target, sem.at[7 + copy, side]))
    for copy in loads + tables:
        copy.start()

    blank = jnp.zeros((MODES, cols), wide_ref.dtype)
    for block in range(6):
        wide_ref[block * MODES : (block + 1) * MODES, (1 - block % 2) * cols : (2 - block % 2) * cols] = blank
    zero = jnp.zeros((SUB, LANES), jnp.float32)
    for item in (1, 3):
        for level in range(levels):
            for tile in range(tiles + 1):
                ext_ref[item, level, tile, pl.ds(0, SUB)] = zero
                ext_ref[item, level, tile, pl.ds(main + rows + SUB, SUB)] = zero

    def place_slabs(odd):
        for phase, slab in enumerate((a_ref, b_ref)):
            base = GUARD if (odd == 1) == (phase == 0) else main + rows
            for item, place, turn in ((3, 0, 0), (1, 1, 0), (0, 2, 0), (2, 2, 4), (4, 3, 0), (5, 3, 4)):
                for level in range(levels):
                    for tile in range(tiles):
                        value = slab[level, place, :, tile * LANES : (tile + 1) * LANES]
                        if turn:
                            value = pltpu.roll(value, turn, 0)
                        ext_ref[item, level, tile, pl.ds(base, SUB)] = value

    for odd in range(2):
        pl.when(facts[6] == odd)(functools.partial(place_slabs, odd))
    edges = 6 * len({0, tiles - 1})
    for copy in loads[:edges]:
        copy.wait()

    lane = lax.broadcasted_iota(jnp.int32, (SUB, LANES), 1)

    def pack_band(band, right):
        def pack_rows(part, _):
            row = pl.multiple_of(part * SUB, SUB)
            packed = [jnp.zeros((SUB, LANES), jnp.float32) for _ in range(2)]
            for item, level, width, group, first in band_lanes(levels):
                tile = ext_ref[item, level, (tiles - 1) * right, pl.ds(row + GUARD, SUB)]
                moved = pltpu.roll(tile, (first + right * width) % LANES, 1)
                packed[group] = jnp.where((lane >= first) & (lane < first + width), moved, packed[group])
            for group in range(2):
                band[pl.ds(row, SUB), group * LANES : (group + 1) * LANES] = packed[group]
            return 0

        lax.fori_loop(0, rows // SUB + 2, pack_rows, 0)

    for index, band in enumerate(bands):
        for right in range(2):
            pl.when((facts[3] ^ index) == right)(functools.partial(pack_band, band, right))
    for copy in loads[edges:] + tables:
        copy.wait()


def substep_kernel(facts, *refs, step, levels, rows, cols):
    bands, ext_ref, d_ref = refs[1:-2], refs[-2], refs[-1]
    tiles = cols // LANES
    chunks = rows // SUB
    lane = lax.broadcasted_iota(jnp.int32, (SUB, LANES), 1)

    def unpack_bands(odd):
        def unpack_rows(part, _):
            row = pl.multiple_of(part * SUB, SUB)
            sources = [
                [band[pl.ds(row, SUB), group * LANES : (group + 1) * LANES] for group in range(2)] for band in bands
            ]
            for item, level, width, group, first in band_lanes(levels):
                value = jnp.zeros((SUB, LANES), jnp.float32)
                for phase, source in enumerate(sources):
                    left = odd if phase == 0 else 1 - odd
                    moved = pltpu.roll(source[group], (2 * LANES - first - left * width) % LANES, 1)
                    value = jnp.where(lane >= LANES - width if left else lane < width, moved, value)
                ext_ref[item, level, tiles, pl.ds(row + GUARD, SUB)] = value
            return 0

        lax.fori_loop(0, chunks + 2, unpack_rows, 0)

    if step == 0:
        for odd in range(2):
            pl.when(facts[5] == odd)(functools.partial(unpack_bands, odd))

    quarter = 0.5 * COURANT
    sides = [jnp.where(facts[place] == 1, 1.0, 0.0) for place in (7, 8, 9, 10)]
    has_left, has_right, has_top, has_bottom = sides
    inner = jnp.where(lane == LANES - 1, has_right, 1.0)
    outer = jnp.where(lane < LANES // 2, has_right, jnp.where(lane == LANES - 1, 1.0, has_left))
    ring = tiles + 1

    def ahead(values, tile, count):
        moved = jnp.where(lane < count, values[(tile + 1) % ring], values[tile])
        return pltpu.roll(moved, LANES - count, 1)

    def behind(values, tile, count):
        moved = jnp.where(lane >= LANES - count, values[(tile - 1) % ring], values[tile])
        return pltpu.roll(moved, count, 1)

    u_ref, v_ref, w_ref, p_ref, t_ref, s_ref = (ext_ref.at[item] for item in range(6))
    first, last = step == 0, step == SUBSTEPS - 1

    def flush(pending):
        for ref, level, tile, here, value in pending:
            ref[level, tile, here] = value

    def winds(chunk, only_v=False):
        row = GUARD + chunk * SUB
        here = pl.ds(row, SUB)
        x_tiles = tiles if last else ring
        limit = {0: has_top, chunks + 1: has_bottom}.get(chunk)
        before = None
        line = None if only_v else [p_ref[0, tile, here] for tile in range(ring)]
        for level in range(levels):
            made = []
            for tile in range(x_tiles):
                slope = p_ref[level, tile, pl.ds(row + 1, SUB)] - p_ref[level, tile, pl.ds(row - 1, SUB)]
                if first:
                    slope = slope * (quarter if limit is None else quarter * limit)
                elif limit is not None:
                    slope = slope * limit
                made.append((v_ref, level, tile, here, v_ref[level, tile, here] - slope))
            if only_v:
                flush(made)
                continue
            old = [u_ref[level, tile, here] for tile in range(ring)]
            fresh = []
            for tile in range(ring):
                slope = ahead(line, tile, 2) - line[tile]
                edge = {tiles - 1: inner, tiles: outer}.get(tile)
                if first:
                    slope = slope * (quarter if edge is None else quarter * edge)
                elif edge is not None:
                    slope = slope * edge
                fresh.append((ahead(old, tile, 1) if first else old[tile]) - slope)
            if last:
                for tile in range(tiles):
                    made.append((u_ref, level, tile, here, behind(fresh, tile, 1)))
                    made.append((d_ref, level, tile, here, fresh[tile] - behind(fresh, tile, 2)))
            else:
                for tile in range(ring):
                    made.append((u_ref, level, tile, here, fresh[tile]))
            after = None
            if level + 1 < levels:
                after = [p_ref[level + 1, tile, here] for tile in range(ring)]
            for tile in range(x_tiles):
                if level == 0:
                    lift = after[tile]
                elif level == levels - 1:
                    lift = -before[tile]
                else:
                    lift = after[tile] - before[tile]
                warm = t_ref[level, tile, here]
                if first:
                    lift, warm = quarter * lift, COURANT * warm
                made.append((w_ref, level, tile, here, w_ref[level, tile, here] - (lift - warm)))
            before, line = line, after
            flush(made)

    def scalars(chunk):
        row = GUARD + chunk * SUB
        here = pl.ds(row, SUB)
        x_tiles = tiles if last else ring
        before, now = None, [w_ref[0, tile, here] for tile in range(x_tiles)]
        for level in range(levels):
            made = []
            line = None if last else [u_ref[level, tile, here] for tile in range(ring)]
            after = None
            if level + 1 < levels:
                after = [w_ref[level + 1, tile, here] for tile in range(x_tiles)]
            for tile in range(x_tiles):
                if last:
                    spread = d_ref[level, tile, here]
                else:
                    spread = line[tile] - behind(line, tile, 2)
                spread += v_ref[level, tile, pl.ds(row + 1, SUB)] - v_ref[level, tile, pl.ds(row - 1, SUB)]
                if level == 0:
                    spread += after[tile]
                elif level == levels - 1:
                    spread -= before[tile]
                else:
                    spread += after[tile] - before[tile]
                press, warm, speed = (ref[level, tile, here] for ref in (p_ref, t_ref, s_ref))
                if first:
                    press, warm, speed = quarter * press, COURANT * warm, (quarter * quarter) * speed
                    made.append((s_ref, level, tile, here, speed))
                press = press - speed * spread
                warm = warm - (COURANT * COURANT) * now[tile]
                if last:
                    press, warm = press * (1.0 / quarter), warm * (1.0 / COURANT)
                made.append((p_ref, level, tile, here, press))
                made.append((t_ref, level, tile, here, warm))
            before, now = now, after
            flush(made)

    if last:
        winds(0, True)
        winds(chunks + 1, True)
    span = range(1, chunks + 1) if last else range(chunks + 2)
    for chunk in span:
        winds(chunk)
    for chunk in span:
        scalars(chunk)


def solution(mesh):
    nx, ny = mesh.shape["gx"], mesh.shape["gy"]
    devices = nx * ny
    stages, middle = stages_of(devices)
    pieces = 1
    for stage in stages:
        pieces *= 1 << len(stage)
    pieces = max(pieces, 2)

    def decode(ref):
        number = ref[0]
        gx, gy = lax.div(number, ny), lax.rem(number, ny)
        mine = 0
        for stage in stages:
            for bit in reversed(stage):
                mine = mine * 2 + ((number >> bit) & 1)
        return (
            gx,
            gy,
            mine,
            (gx + 1) % 2,
            (gy + 1) % 2,
            gx % 2,
            gy % 2,
            jnp.where(gx > 0, 1, 0),
            jnp.where(gx < nx - 1, 1, 0),
            jnp.where(gy > 0, 1, 0),
            jnp.where(gy < ny - 1, 1, 0),
        )

    def informed(kernel, **static):
        def body(info, *refs):
            return kernel(decode(info), *refs, **static)

        return body

    x_phases = 1 if nx == 2 else 2

    def swap(value, mask):
        return lax.ppermute(value, ("gx", "gy"), [(i, i ^ mask) for i in range(devices)])

    def neighbours(value, axis, count, phase):
        pairs = []
        for low in range(phase, count - 1, 2):
            pairs += [(low, low + 1), (low + 1, low)]
        return lax.ppermute(value, axis, pairs)

    def on_device(state, driving, rate, sound_square):
        fields, levels, rows, cols = state.shape
        half = levels // 2
        chunk = half * MODES // pieces
        info = (lax.axis_index("gx") * ny + lax.axis_index("gy")).reshape(1)

        basis_x, weight_x = bases(MODES, cols * nx)
        basis_y, weight_y = bases(MODES, rows * ny)
        high, low = halves(weight_x)
        wx = np.concatenate([high, low], axis=0).T.reshape(nx, cols, 2 * MODES)
        high, low = halves(weight_y)
        wy = np.concatenate([high, low], axis=0).reshape(2 * MODES, ny, rows).transpose(1, 0, 2)
        high, low = halves(basis_x)
        bx = np.stack([high, low]).reshape(2, MODES, nx, cols).transpose(2, 0, 1, 3)
        high, low = halves(basis_y)
        by = np.stack([high, low]).reshape(2, MODES, ny, rows).transpose(2, 0, 3, 1).reshape(ny, 2 * rows, MODES)
        wx, wy, bx, by = (jnp.asarray(np.ascontiguousarray(t)) for t in (wx, wy, bx, by))

        hbm = pl.BlockSpec(memory_space=pltpu.HBM)
        vmem = pl.BlockSpec(memory_space=pltpu.VMEM)

        def call(kernel, name, shapes, ins, scratch, operands, flops=0, data=0, prefetch=1, aliases=None):
            return pl.pallas_call(
                kernel,
                grid_spec=pltpu.PrefetchScalarGridSpec(
                    num_scalar_prefetch=prefetch,
                    grid=(),
                    in_specs=ins,
                    out_specs=[vmem if name != "nudge" else hbm for _ in shapes],
                    scratch_shapes=scratch,
                ),
                out_shape=shapes,
                input_output_aliases=aliases or {},
                compiler_params=pltpu.CompilerParams(vmem_limit_bytes=VMEM_LIMIT),
                cost_estimate=pl.CostEstimate(flops=flops, bytes_accessed=data, transcendentals=0),
            )(*operands)

        def array(shape, dtype=jnp.float32):
            return jax.ShapeDtypeStruct(shape, dtype)

        tiles = cols // LANES
        slab_shape = (levels, 4, SUB, cols)
        slab_a, slab_b = call(
            informed(slab_kernel),
            "slabs",
            [array(slab_shape)] * 2,
            [hbm, hbm],
            [pltpu.VMEM((2, 2, levels, SUB, cols), jnp.float32), pltpu.SemaphoreType.DMA((2, 6))],
            (info, state, sound_square),
        )
        slab_a = neighbours(slab_a, "gy", ny, 0)
        slab_b = neighbours(slab_b, "gy", ny, 1)

        piece_shape = (pieces // 2, fields, chunk, LANES)
        keep, send = call(
            informed(project_kernel),
            "project",
            [array(piece_shape)] * 2,
            [hbm] * 4,
            [
                pltpu.VMEM((fields, levels, rows, cols), jnp.float32),
                pltpu.VMEM((fields, levels, rows, cols), jnp.float32),
                pltpu.VMEM((cols, 2 * MODES), jnp.bfloat16),
                pltpu.VMEM((2 * MODES, rows), jnp.bfloat16),
                pltpu.VMEM((fields, half * rows, 2 * LANES), jnp.bfloat16),
                pltpu.VMEM((fields, half * MODES, LANES), jnp.float32),
                pltpu.SemaphoreType.DMA((fields + 1, 2)),
            ],
            (info, state, driving, wx, wy),
            600_000_000,
            8_500_000,
        )

        ext_shape = (6, levels, tiles + 1, rows + 2 * SUB + 2 * GUARD, LANES)
        band_shape = (rows + 2 * SUB, 2 * LANES)
        ext, wide, back, *bands = call(
            informed(load_kernel),
            "load",
            [
                array(ext_shape),
                array((6 * MODES, 2 * cols), jnp.bfloat16),
                array((2 * rows, MODES), jnp.bfloat16),
            ]
            + [array(band_shape)] * x_phases,
            [hbm, hbm, vmem, vmem, hbm, hbm],
            [pltpu.SemaphoreType.DMA((10, max(tiles, 2)))],
            (info, state, sound_square, slab_a, slab_b, bx, by),
            1_000_000,
            10_000_000,
        )
        bands = [neighbours(band, "gx", nx, index) for index, band in enumerate(bands)]

        for step in range(SUBSTEPS):
            extra = bands if step == 0 else []
            (ext,) = call(
                informed(substep_kernel, step=step, levels=levels, rows=rows, cols=cols),
                f"substep_{step}",
                [array(ext_shape)],
                [vmem] * (1 + len(extra)),
                [pltpu.VMEM(ext_shape[1:], jnp.float32)],
                (info, ext, *extra),
                10_000_000,
                8_000_000,
                aliases={1: 0},
            )

        value = None
        for place, stage in enumerate(stages):
            masks = masks_of(stage)
            if place == 0:
                value = keep + swap(send, masks[1])
                continue
            value = value.reshape((len(masks), value.shape[0] // len(masks)) + value.shape[1:])
            moved = [swap(value[i], masks[i]) for i in range(1, len(masks))]
            value = functools.reduce(jnp.add, moved, value[0])
        moved = [swap(value, mask) for i, mask in enumerate(masks_of(middle)) if i]
        value = functools.reduce(jnp.add, moved, value)
        for place in reversed(range(1, len(stages))):
            moved = [swap(value, mask) for i, mask in enumerate(masks_of(stages[place])) if i]
            value = jnp.concatenate([value] + moved, axis=0)
        far = swap(value, masks_of(stages[0])[1])

        (out,) = call(
            informed(nudge_kernel),
            "nudge",
            [array(state.shape)],
            [vmem] * 5,
            [
                pltpu.VMEM((fields, half * MODES, LANES), jnp.float32),
                pltpu.VMEM((fields, half * rows, 2 * LANES), jnp.bfloat16),
                pltpu.VMEM((fields, levels, rows, cols), jnp.float32),
                pltpu.SemaphoreType.DMA((fields,)),
            ],
            (info, rate, ext, value, far, wide, back),
            600_000_000,
            8_500_000,
            prefetch=2,
        )
        return out

    return jax.shard_map(
        on_device,
        mesh=mesh,
        in_specs=(P(None, None, "gy", "gx"), P(None, None, "gy", "gx"), P(), P(None, "gy", "gx")),
        out_specs=P(None, None, "gy", "gx"),
        check_vma=False,
    )
```

```python
import functools

import jax
import jax.numpy as jnp
import numpy as np
from jax import lax
from jax.experimental import pallas as pl
from jax.experimental.pallas import tpu as pltpu
from jax.sharding import PartitionSpec as P


MODES = 64
SUBSTEPS = 3
COURANT = 0.5
LANES = 128
SUB = 8
GUARD = 8
VMEM_LIMIT = 32 << 20

REACH_X = (5, 4, 4, 6, 4, 4)
GROUP_X = (0, 0, 1, 0, 1, 1)


def lane_starts(levels):
    used = [0, 0]
    starts = []
    for width, group in zip(REACH_X, GROUP_X):
        starts.append(used[group])
        used[group] += width * levels
    assert max(used) <= LANES
    return starts


def bases(count, total):
    index = np.arange(total, dtype=np.int64)
    order = np.arange(count, dtype=np.int64)
    freq = np.where(order < count // 2, order, order - count // 2 + 1)
    wrapped = (freq[:, None] * (2 * index[None, :] + 1)) % (2 * total)
    phase = np.pi * wrapped.astype(np.float64) / total
    basis = np.where(order[:, None] < count // 2, np.cos(phase), np.sin(phase))
    scaling = np.where(order == 0, 1.0 / total, 2.0 / total)
    basis32 = basis.astype(np.float32)
    weight32 = (basis * scaling[:, None]).astype(np.float32)
    return basis32, weight32


def halves(table):
    high = table.astype(jnp.bfloat16)
    low = (table - high.astype(np.float32)).astype(jnp.bfloat16)
    return np.asarray(high), np.asarray(low)


def split(value):
    high = value.astype(jnp.bfloat16)
    low = (value - high.astype(jnp.float32)).astype(jnp.bfloat16)
    return high, low


def dot(left, right):
    return jnp.dot(left, right, preferred_element_type=jnp.float32)


def masks_of(bits):
    masks = [0]
    for bit in bits:
        masks = masks + [mask | (1 << bit) for mask in masks]
    return masks


def stages_of(devices):
    total = devices.bit_length() - 1
    assert devices == 1 << total
    left = list(range(total))
    stages = []
    if left:
        stages.append([left.pop(0)])
    while len(left) > 3 and len(stages) < 3:
        stages.append([left.pop(0), left.pop()])
    return stages, left


def head_kernel(
    facts,
    state_ref,
    driving_ref,
    sound_ref,
    wx_hbm,
    wy_hbm,
    ext_ref,
    a_ref,
    b_ref,
    keep_ref,
    send_ref,
    other_ref,
    wx_ref,
    wy_ref,
    packed_ref,
    modes_ref,
    sem,
):
    fields, levels, rows, cols = state_ref.shape
    tiles = cols // LANES
    half = levels // 2
    pieces = 2 * keep_ref.shape[0]
    chunk = keep_ref.shape[2]
    main = pl.ds(GUARD + SUB, rows)

    def fetch(item):
        source = state_ref.at[item] if item < fields else sound_ref
        copies = [
            pltpu.make_async_copy(
                source.at[:, :, pl.ds(tile * LANES, LANES)], ext_ref.at[item, :, tile, main], sem.at[item, tile]
            )
            for tile in range(tiles)
        ]
        if item < fields:
            copies.append(pltpu.make_async_copy(driving_ref.at[item], other_ref.at[item], sem.at[item, tiles]))
        return copies

    tables = [
        pltpu.make_async_copy(wx_hbm.at[facts[0]], wx_ref, sem.at[fields + 1, 0]),
        pltpu.make_async_copy(wy_hbm.at[facts[1]], wy_ref, sem.at[fields + 1, 1]),
    ]
    loads = [fetch(item) for item in range(fields + 1)]
    for copy in [*tables, *(copy for load in loads for copy in load)]:
        copy.start()
    lane = lax.broadcasted_iota(jnp.int32, (half * rows, LANES), 1)
    for copy in tables:
        copy.wait()
    weights = wx_ref[...]

    def rows_of(field):
        for pair in range(half):
            out = dot(wy_ref[...], packed_ref[field, pair * rows : (pair + 1) * rows])
            out = out[:MODES] + out[MODES:]
            modes_ref[field, pair * MODES : (pair + 1) * MODES] = out[:, :LANES] + out[:, LANES:]

    for field in range(fields):
        for copy in loads[field]:
            copy.wait()
        sides = []
        for side in range(2):
            part = pl.ds(side * half, half)
            tile_of = [ext_ref[field, part, tile, main].reshape(half * rows, LANES) for tile in range(tiles)]
            diff = jnp.concatenate(tile_of, axis=1) - other_ref[field, part].reshape(half * rows, cols)
            high, low = split(diff)
            both = dot(high, weights) + dot(low, weights)
            sides.append(both + pltpu.roll(both, MODES, 1))
        high, low = split(jnp.where(lane < MODES, sides[0], sides[1]))
        packed_ref[field, :, :LANES] = high
        packed_ref[field, :, LANES:] = low
        if field:
            rows_of(field - 1)
    for copy in loads[fields]:
        copy.wait()
    rows_of(fields - 1)
    mine = facts[2]
    for piece in range(pieces):
        source = pl.multiple_of(jnp.bitwise_xor(mine, piece) * chunk, SUB)
        target = keep_ref if piece < pieces // 2 else send_ref
        target[piece % (pieces // 2)] = modes_ref[:, pl.ds(source, chunk)]

    upper = lax.broadcasted_iota(jnp.int32, (SUB, LANES), 0) >= 4

    def pack(bottom):
        for out_ref, last in ((a_ref, bottom), (b_ref, 1 - bottom)):
            here = pl.ds(GUARD + SUB + last * (rows - SUB), SUB)
            for level in range(levels):
                for tile in range(tiles):
                    lanes = pl.ds(tile * LANES, LANES)
                    u, v, w, p, t, s = (ext_ref[item, level, tile, here] for item in range(6))
                    out_ref[level, 0, :, lanes] = p
                    out_ref[level, 1, :, lanes] = v
                    for place, own, more in ((2, u, w), (3, t, s)):
                        more = pltpu.roll(more, 4, 0)
                        out_ref[level, place, :, lanes] = jnp.where(upper, own, more) if last else jnp.where(upper, more, own)

    for bottom in range(2):
        pl.when(facts[4] == bottom)(functools.partial(pack, bottom))


def nudge_kernel(facts, rate_ref, ext_ref, own_ref, far_ref, wide_ref, by_ref, out_ref, modes_ref, back_ref, done_ref, sem):
    fields, levels, rows, cols = out_ref.shape
    tiles = cols // LANES
    half = levels // 2
    pieces = 2 * own_ref.shape[0]
    chunk = own_ref.shape[2]
    mine = facts[2]
    for piece in range(pieces):
        target = pl.multiple_of(jnp.bitwise_xor(mine, piece) * chunk, SUB)
        source = own_ref if piece < pieces // 2 else far_ref
        modes_ref[:, pl.ds(target, chunk)] = source[piece % (pieces // 2)]
    lane = lax.broadcasted_iota(jnp.int32, (MODES, LANES), 1)
    for field in range(fields):
        for pair in range(half):
            factor = jnp.where(lane < MODES, rate_ref[field, pair], rate_ref[field, pair + half])
            high, low = split(modes_ref[field, pair * MODES : (pair + 1) * MODES] * factor)
            out = dot(by_ref[...], jnp.concatenate([high, low], axis=1))
            out = out[:rows] + out[rows:]
            high, low = split(out[:, :LANES] + out[:, LANES:])
            back_ref[field, pair * rows : (pair + 1) * rows, :LANES] = high
            back_ref[field, pair * rows : (pair + 1) * rows, LANES:] = low
    main = pl.ds(GUARD + SUB, rows)
    last_lane = lax.broadcasted_iota(jnp.int32, (rows, LANES), 1) == LANES - 1
    stores = []
    for field in range(fields):
        left = back_ref[field]
        tendency = dot(left, wide_ref[: 4 * MODES]) + dot(left[:, :LANES], wide_ref[4 * MODES :])
        for level in range(levels):
            first = (level % half) * rows
            for tile in range(tiles):
                lanes = pl.ds(tile * LANES, LANES)
                column = (level // half) * cols + tile * LANES
                value = ext_ref[field, level, tile, main]
                if field == 0:
                    before = ext_ref[field, level, (tile - 1) % (tiles + 1), main]
                    value = pltpu.roll(jnp.where(last_lane, before, value), 1, 1)
                done_ref[field, level, :, lanes] = value - tendency[first : first + rows, column : column + LANES]
            if level % half == half - 1:
                part = pl.ds(level + 1 - half, half)
                place = sem.at[field, level // half]
                stores.append(pltpu.make_async_copy(done_ref.at[field, part], out_ref.at[field, part], place))
                stores[-1].start()
    for copy in stores:
        copy.wait()


def band_lanes(level_count):
    starts = lane_starts(level_count)
    for item in range(6):
        for level in range(level_count):
            yield item, level, REACH_X[item], GROUP_X[item], starts[item] + REACH_X[item] * level


def band_kernel(facts, _, a_ref, b_ref, bx_hbm, by_hbm, ext_ref, wide_ref, by_ref, *refs, rows, cols):
    *bands, sem = refs
    levels = ext_ref.shape[1]
    tiles = cols // LANES
    main = GUARD + SUB
    tables = [pltpu.make_async_copy(by_hbm.at[facts[1]], by_ref, sem.at[3, 0])]
    for copy in range(3):
        for side in range(2):
            target = wide_ref.at[pl.ds((2 * copy + side) * MODES, MODES), pl.ds(side * cols, cols)]
            tables.append(pltpu.make_async_copy(bx_hbm.at[facts[0], copy // 2], target, sem.at[copy, side]))
    for copy in tables:
        copy.start()

    blank = jnp.zeros((MODES, cols), wide_ref.dtype)
    for block in range(6):
        wide_ref[block * MODES : (block + 1) * MODES, (1 - block % 2) * cols : (2 - block % 2) * cols] = blank
    zero = jnp.zeros((SUB, LANES), jnp.float32)
    for item in (1, 3):
        for level in range(levels):
            for tile in range(tiles + 1):
                ext_ref[item, level, tile, pl.ds(0, SUB)] = zero
                ext_ref[item, level, tile, pl.ds(main + rows + SUB, SUB)] = zero

    def place_slabs(odd):
        for phase, slab in enumerate((a_ref, b_ref)):
            base = GUARD if (odd == 1) == (phase == 0) else main + rows
            for item, place, turn in ((3, 0, 0), (1, 1, 0), (0, 2, 0), (2, 2, 4), (4, 3, 0), (5, 3, 4)):
                for level in range(levels):
                    for tile in range(tiles):
                        value = slab[level, place, :, tile * LANES : (tile + 1) * LANES]
                        if turn:
                            value = pltpu.roll(value, turn, 0)
                        ext_ref[item, level, tile, pl.ds(base, SUB)] = value

    for odd in range(2):
        pl.when(facts[6] == odd)(functools.partial(place_slabs, odd))
    lane = lax.broadcasted_iota(jnp.int32, (SUB, LANES), 1)

    def pack_band(band, right):
        def pack_rows(part, _):
            row = pl.multiple_of(part * SUB, SUB)
            packed = [jnp.zeros((SUB, LANES), jnp.float32) for _ in range(2)]
            for item, level, width, group, first in band_lanes(levels):
                tile = ext_ref[item, level, (tiles - 1) * right, pl.ds(row + GUARD, SUB)]
                moved = pltpu.roll(tile, (first + right * width) % LANES, 1)
                packed[group] = jnp.where((lane >= first) & (lane < first + width), moved, packed[group])
            for group in range(2):
                band[pl.ds(row, SUB), group * LANES : (group + 1) * LANES] = packed[group]
            return 0

        lax.fori_loop(0, rows // SUB + 2, pack_rows, 0)

    for index, band in enumerate(bands):
        for right in range(2):
            pl.when((facts[3] ^ index) == right)(functools.partial(pack_band, band, right))
    for copy in tables:
        copy.wait()


def substep_kernel(facts, *refs, step, levels, rows, cols):
    bands, ext_ref = refs[1:-1], refs[-1]
    tiles = cols // LANES
    chunks = rows // SUB
    lane = lax.broadcasted_iota(jnp.int32, (SUB, LANES), 1)

    def unpack_bands(odd):
        def unpack_rows(part, _):
            row = pl.multiple_of(part * SUB, SUB)
            sources = [
                [band[pl.ds(row, SUB), group * LANES : (group + 1) * LANES] for group in range(2)] for band in bands
            ]
            for item, level, width, group, first in band_lanes(levels):
                value = jnp.zeros((SUB, LANES), jnp.float32)
                for phase, source in enumerate(sources):
                    left = odd if phase == 0 else 1 - odd
                    moved = pltpu.roll(source[group], (2 * LANES - first - left * width) % LANES, 1)
                    value = jnp.where(lane >= LANES - width if left else lane < width, moved, value)
                ext_ref[item, level, tiles, pl.ds(row + GUARD, SUB)] = value
            return 0

        lax.fori_loop(0, chunks + 2, unpack_rows, 0)

    if step == 0:
        for odd in range(2):
            pl.when(facts[5] == odd)(functools.partial(unpack_bands, odd))

    quarter = 0.5 * COURANT
    sides = [jnp.where(facts[place] == 1, 1.0, 0.0) for place in (7, 8, 9, 10)]
    has_left, has_right, has_top, has_bottom = sides
    inner = jnp.where(lane == LANES - 1, has_right, 1.0)
    outer = jnp.where(lane < LANES // 2, has_right, jnp.where(lane == LANES - 1, 1.0, has_left))
    ring = tiles + 1

    def ahead(values, tile, count):
        moved = jnp.where(lane < count, values[(tile + 1) % ring], values[tile])
        return pltpu.roll(moved, LANES - count, 1)

    def behind(values, tile, count):
        moved = jnp.where(lane >= LANES - count, values[(tile - 1) % ring], values[tile])
        return pltpu.roll(moved, count, 1)

    u_ref, v_ref, w_ref, p_ref, t_ref, s_ref = (ext_ref.at[item] for item in range(6))
    first, last = step == 0, step == SUBSTEPS - 1

    def flush(pending):
        for ref, level, tile, here, value in pending:
            ref[level, tile, here] = value

    def winds(chunk, only_v=False):
        row = GUARD + chunk * SUB
        here = pl.ds(row, SUB)
        x_tiles = tiles if last else ring
        limit = {0: has_top, chunks + 1: has_bottom}.get(chunk)
        before = None
        line = None if only_v else [p_ref[0, tile, here] for tile in range(ring)]
        for level in range(levels):
            made = []
            for tile in range(x_tiles):
                slope = p_ref[level, tile, pl.ds(row + 1, SUB)] - p_ref[level, tile, pl.ds(row - 1, SUB)]
                if first:
                    slope = slope * (quarter if limit is None else quarter * limit)
                elif limit is not None:
                    slope = slope * limit
                made.append((v_ref, level, tile, here, v_ref[level, tile, here] - slope))
            if only_v:
                flush(made)
                continue
            old = [u_ref[level, tile, here] for tile in range(ring)]
            fresh = []
            for tile in range(ring):
                slope = ahead(line, tile, 2) - line[tile]
                edge = {tiles - 1: inner, tiles: outer}.get(tile)
                if first:
                    slope = slope * (quarter if edge is None else quarter * edge)
                elif edge is not None:
                    slope = slope * edge
                fresh.append(old[tile] - slope)
            for tile in range(ring):
                made.append((u_ref, level, tile, here, fresh[tile]))
            after = None
            if level + 1 < levels:
                after = [p_ref[level + 1, tile, here] for tile in range(ring)]
            for tile in range(x_tiles):
                if level == 0:
                    lift = after[tile]
                elif level == levels - 1:
                    lift = -before[tile]
                else:
                    lift = after[tile] - before[tile]
                warm = t_ref[level, tile, here]
                if first:
                    lift, warm = quarter * lift, COURANT * warm
                made.append((w_ref, level, tile, here, w_ref[level, tile, here] - (lift - warm)))
            before, line = line, after
            flush(made)

    def scalars(chunk):
        row = GUARD + chunk * SUB
        here = pl.ds(row, SUB)
        x_tiles = tiles if last else ring
        before, now = None, [w_ref[0, tile, here] for tile in range(x_tiles)]
        for level in range(levels):
            made = []
            line = [u_ref[level, tile, here] for tile in range(ring)]
            after = None
            if level + 1 < levels:
                after = [w_ref[level + 1, tile, here] for tile in range(x_tiles)]
            for tile in range(x_tiles):
                spread = line[tile] - behind(line, tile, 2)
                spread += v_ref[level, tile, pl.ds(row + 1, SUB)] - v_ref[level, tile, pl.ds(row - 1, SUB)]
                if level == 0:
                    spread += after[tile]
                elif level == levels - 1:
                    spread -= before[tile]
                else:
                    spread += after[tile] - before[tile]
                press, warm, speed = (ref[level, tile, here] for ref in (p_ref, t_ref, s_ref))
                if first:
                    press, warm, speed = quarter * press, COURANT * warm, (quarter * quarter) * speed
                    made.append((s_ref, level, tile, here, speed))
                press = press - speed * spread
                warm = warm - (COURANT * COURANT) * now[tile]
                if last:
                    press, warm = press * (1.0 / quarter), warm * (1.0 / COURANT)
                made.append((p_ref, level, tile, here, press))
                made.append((t_ref, level, tile, here, warm))
            before, now = now, after
            flush(made)

    def shift_rows(part, _):
        here = pl.ds(pl.multiple_of(part * SUB, SUB) + GUARD, SUB)
        for level in range(levels):
            old = [u_ref[level, tile, here] for tile in range(ring)]
            for tile in range(ring):
                u_ref[level, tile, here] = ahead(old, tile, 1)
        return 0

    if first:
        lax.fori_loop(0, chunks + 2, shift_rows, 0)
    if last:
        winds(0, True)
        winds(chunks + 1, True)
    span = range(1, chunks + 1) if last else range(chunks + 2)
    for chunk in span:
        winds(chunk)
    for chunk in span:
        scalars(chunk)


def solution(mesh):
    nx, ny = mesh.shape["gx"], mesh.shape["gy"]
    devices = nx * ny
    stages, middle = stages_of(devices)
    pieces = 1
    for stage in stages:
        pieces *= 1 << len(stage)
    pieces = max(pieces, 2)

    def decode(ref):
        number = ref[0]
        gx, gy = lax.div(number, ny), lax.rem(number, ny)
        mine = 0
        for stage in stages:
            for bit in reversed(stage):
                mine = mine * 2 + ((number >> bit) & 1)
        return (
            gx,
            gy,
            mine,
            (gx + 1) % 2,
            (gy + 1) % 2,
            gx % 2,
            gy % 2,
            jnp.where(gx > 0, 1, 0),
            jnp.where(gx < nx - 1, 1, 0),
            jnp.where(gy > 0, 1, 0),
            jnp.where(gy < ny - 1, 1, 0),
        )

    def informed(kernel, **static):
        def body(info, *refs):
            return kernel(decode(info), *refs, **static)

        return body

    x_phases = 1 if nx == 2 else 2

    def swap(value, mask):
        return lax.ppermute(value, ("gx", "gy"), [(i, i ^ mask) for i in range(devices)])

    def neighbours(value, axis, count, phase):
        pairs = []
        for low in range(phase, count - 1, 2):
            pairs += [(low, low + 1), (low + 1, low)]
        return lax.ppermute(value, axis, pairs)

    def on_device(state, driving, rate, sound_square):
        fields, levels, rows, cols = state.shape
        half = levels // 2
        chunk = half * MODES // pieces
        info = (lax.axis_index("gx") * ny + lax.axis_index("gy")).reshape(1)

        basis_x, weight_x = bases(MODES, cols * nx)
        basis_y, weight_y = bases(MODES, rows * ny)
        high, low = halves(weight_x)
        wx = np.concatenate([high, low], axis=0).T.reshape(nx, cols, 2 * MODES)
        high, low = halves(weight_y)
        wy = np.concatenate([high, low], axis=0).reshape(2 * MODES, ny, rows).transpose(1, 0, 2)
        high, low = halves(basis_x)
        bx = np.stack([high, low]).reshape(2, MODES, nx, cols).transpose(2, 0, 1, 3)
        high, low = halves(basis_y)
        by = np.stack([high, low]).reshape(2, MODES, ny, rows).transpose(2, 0, 3, 1).reshape(ny, 2 * rows, MODES)
        wx, wy, bx, by = (jnp.asarray(np.ascontiguousarray(t)) for t in (wx, wy, bx, by))

        hbm = pl.BlockSpec(memory_space=pltpu.HBM)
        vmem = pl.BlockSpec(memory_space=pltpu.VMEM)

        def call(kernel, name, shapes, ins, scratch, operands, flops=0, data=0, prefetch=1, aliases=None, limit=VMEM_LIMIT):
            return pl.pallas_call(
                kernel,
                grid_spec=pltpu.PrefetchScalarGridSpec(
                    num_scalar_prefetch=prefetch,
                    grid=(),
                    in_specs=ins,
                    out_specs=[vmem if name != "nudge" else hbm for _ in shapes],
                    scratch_shapes=scratch,
                ),
                out_shape=shapes,
                input_output_aliases=aliases or {},
                compiler_params=pltpu.CompilerParams(vmem_limit_bytes=limit),
                cost_estimate=pl.CostEstimate(flops=flops, bytes_accessed=data, transcendentals=0),
            )(*operands)

        def array(shape, dtype=jnp.float32):
            return jax.ShapeDtypeStruct(shape, dtype)

        tiles = cols // LANES
        slab_shape = (levels, 4, SUB, cols)
        piece_shape = (pieces // 2, fields, chunk, LANES)
        ext_shape = (6, levels, tiles + 1, rows + 2 * SUB + 2 * GUARD, LANES)
        band_shape = (rows + 2 * SUB, 2 * LANES)
        ext, slab_a, slab_b, keep, send = call(
            informed(head_kernel),
            "head",
            [array(ext_shape), *[array(slab_shape)] * 2, *[array(piece_shape)] * 2],
            [hbm] * 5,
            [
                pltpu.VMEM((fields, levels, rows, cols), jnp.float32),
                pltpu.VMEM((cols, 2 * MODES), jnp.bfloat16),
                pltpu.VMEM((2 * MODES, rows), jnp.bfloat16),
                pltpu.VMEM((fields, half * rows, 2 * LANES), jnp.bfloat16),
                pltpu.VMEM((fields, half * MODES, LANES), jnp.float32),
                pltpu.SemaphoreType.DMA((fields + 2, tiles + 1)),
            ],
            (info, *(pltpu.with_memory_space_constraint(x, pltpu.HBM) for x in (state, driving, sound_square, wx, wy))),
            600_000_000,
            9_000_000,
        )
        slab_a = neighbours(slab_a, "gy", ny, 0)
        slab_b = neighbours(slab_b, "gy", ny, 1)

        ext, wide, back, *bands = call(
            informed(band_kernel, rows=rows, cols=cols),
            "band",
            [
                array(ext_shape),
                array((6 * MODES, 2 * cols), jnp.bfloat16),
                array((2 * rows, MODES), jnp.bfloat16),
            ]
            + [array(band_shape)] * x_phases,
            [vmem, vmem, vmem, hbm, hbm],
            [pltpu.SemaphoreType.DMA((4, 2))],
            (info, ext, slab_a, slab_b, bx, by),
            1_000_000,
            10_000_000,
            aliases={1: 0},
        )
        bands = [neighbours(band, "gx", nx, index) for index, band in enumerate(bands)]

        for step in range(SUBSTEPS):
            extra = bands if step == 0 else []
            (ext,) = call(
                informed(substep_kernel, step=step, levels=levels, rows=rows, cols=cols),
                f"substep_{step}",
                [array(ext_shape)],
                [vmem] * (1 + len(extra)),
                [],
                (info, ext, *extra),
                10_000_000,
                8_000_000,
                aliases={1: 0},
            )

        value = None
        for place, stage in enumerate(stages):
            masks = masks_of(stage)
            if place == 0:
                value = keep + swap(send, masks[1])
                continue
            value = value.reshape((len(masks), value.shape[0] // len(masks)) + value.shape[1:])
            moved = [swap(value[i], masks[i]) for i in range(1, len(masks))]
            value = functools.reduce(jnp.add, moved, value[0])
        moved = [swap(value, mask) for i, mask in enumerate(masks_of(middle)) if i]
        value = functools.reduce(jnp.add, moved, value)
        for place in reversed(range(1, len(stages))):
            moved = [swap(value, mask) for i, mask in enumerate(masks_of(stages[place])) if i]
            value = jnp.concatenate([value] + moved, axis=0)
        far = swap(value, masks_of(stages[0])[1])

        (out,) = call(
            informed(nudge_kernel),
            "nudge",
            [array(state.shape)],
            [vmem] * 5,
            [
                pltpu.VMEM((fields, half * MODES, LANES), jnp.float32),
                pltpu.VMEM((fields, half * rows, 2 * LANES), jnp.bfloat16),
                pltpu.VMEM((fields, levels, rows, cols), jnp.float32),
                pltpu.SemaphoreType.DMA((fields, 2)),
            ],
            (info, rate, ext, value, far, wide, back),
            600_000_000,
            8_500_000,
            prefetch=2,
        )
        return out

    return jax.shard_map(
        on_device,
        mesh=mesh,
        in_specs=(P(None, None, "gy", "gx"), P(None, None, "gy", "gx"), P(), P(None, "gy", "gx")),
        out_specs=P(None, None, "gy", "gx"),
        check_vma=False,
    )
```

```python
import functools

import jax
import jax.numpy as jnp
import numpy as np
from jax import lax
from jax.experimental import pallas as pl
from jax.experimental.pallas import tpu as pltpu
from jax.sharding import PartitionSpec as P


MODES = 64
SUBSTEPS = 3
COURANT = 0.5
LANES = 128
SUB = 8
GUARD = 8
VMEM_LIMIT = 32 << 20

REACH_X = (5, 4, 4, 6, 4, 4)
GROUP_X = (0, 0, 1, 0, 1, 1)


def lane_starts(levels):
    used = [0, 0]
    starts = []
    for width, group in zip(REACH_X, GROUP_X):
        starts.append(used[group])
        used[group] += width * levels
    assert max(used) <= LANES
    return starts


def bases(count, total):
    index = np.arange(total, dtype=np.int64)
    order = np.arange(count, dtype=np.int64)
    freq = np.where(order < count // 2, order, order - count // 2 + 1)
    wrapped = (freq[:, None] * (2 * index[None, :] + 1)) % (2 * total)
    phase = np.pi * wrapped.astype(np.float64) / total
    basis = np.where(order[:, None] < count // 2, np.cos(phase), np.sin(phase))
    scaling = np.where(order == 0, 1.0 / total, 2.0 / total)
    basis32 = basis.astype(np.float32)
    weight32 = (basis * scaling[:, None]).astype(np.float32)
    return basis32, weight32


def halves(table):
    high = table.astype(jnp.bfloat16)
    low = (table - high.astype(np.float32)).astype(jnp.bfloat16)
    return np.asarray(high), np.asarray(low)


def split(value):
    high = value.astype(jnp.bfloat16)
    low = (value - high.astype(jnp.float32)).astype(jnp.bfloat16)
    return high, low


def dot(left, right):
    return jnp.dot(left, right, preferred_element_type=jnp.float32)


def masks_of(bits):
    masks = [0]
    for bit in bits:
        masks = masks + [mask | (1 << bit) for mask in masks]
    return masks


def stages_of(devices):
    total = devices.bit_length() - 1
    assert devices == 1 << total
    left = list(range(total))
    stages = []
    if left:
        stages.append([left.pop(0)])
    while len(left) > 3 and len(stages) < 3:
        stages.append([left.pop(0), left.pop()])
    return stages, left


def head_kernel(
    facts,
    state_ref,
    driving_ref,
    sound_ref,
    wx_hbm,
    wy_hbm,
    ext_ref,
    a_ref,
    b_ref,
    keep_ref,
    send_ref,
    other_ref,
    wx_ref,
    wy_ref,
    packed_ref,
    modes_ref,
    sem,
):
    fields, levels, rows, cols = state_ref.shape
    tiles = cols // LANES
    half = levels // 2
    pieces = 2 * keep_ref.shape[0]
    chunk = keep_ref.shape[2]
    main = pl.ds(GUARD + SUB, rows)

    def fetch(item):
        source = state_ref.at[item] if item < fields else sound_ref
        copies = [
            pltpu.make_async_copy(
                source.at[:, :, pl.ds(tile * LANES, LANES)], ext_ref.at[item, :, tile, main], sem.at[item, tile]
            )
            for tile in range(tiles)
        ]
        if item < fields:
            copies.append(pltpu.make_async_copy(driving_ref.at[item], other_ref.at[item], sem.at[item, tiles]))
        return copies

    tables = [
        pltpu.make_async_copy(wx_hbm.at[facts[0]], wx_ref, sem.at[fields + 1, 0]),
        pltpu.make_async_copy(wy_hbm.at[facts[1]], wy_ref, sem.at[fields + 1, 1]),
    ]
    loads = [fetch(item) for item in range(fields + 1)]
    for copy in [*tables, *(copy for load in loads for copy in load)]:
        copy.start()
    lane = lax.broadcasted_iota(jnp.int32, (half * rows, LANES), 1)
    for copy in tables:
        copy.wait()
    weights = wx_ref[...]

    def rows_of(field):
        for pair in range(half):
            out = dot(wy_ref[...], packed_ref[field, pair * rows : (pair + 1) * rows])
            out = out[:MODES] + out[MODES:]
            modes_ref[field, pair * MODES : (pair + 1) * MODES] = out[:, :LANES] + out[:, LANES:]

    for field in range(fields):
        for copy in loads[field]:
            copy.wait()
        sides = []
        for side in range(2):
            part = pl.ds(side * half, half)
            tile_of = [ext_ref[field, part, tile, main].reshape(half * rows, LANES) for tile in range(tiles)]
            diff = jnp.concatenate(tile_of, axis=1) - other_ref[field, part].reshape(half * rows, cols)
            high, low = split(diff)
            both = dot(high, weights) + dot(low, weights)
            sides.append(both + pltpu.roll(both, MODES, 1))
        high, low = split(jnp.where(lane < MODES, sides[0], sides[1]))
        packed_ref[field, :, :LANES] = high
        packed_ref[field, :, LANES:] = low
        if field:
            rows_of(field - 1)
    for copy in loads[fields]:
        copy.wait()
    rows_of(fields - 1)
    mine = facts[2]
    for piece in range(pieces):
        source = pl.multiple_of(jnp.bitwise_xor(mine, piece) * chunk, SUB)
        target = keep_ref if piece < pieces // 2 else send_ref
        target[piece % (pieces // 2)] = modes_ref[:, pl.ds(source, chunk)]

    upper = lax.broadcasted_iota(jnp.int32, (SUB, LANES), 0) >= 4

    def pack(bottom):
        for out_ref, last in ((a_ref, bottom), (b_ref, 1 - bottom)):
            here = pl.ds(GUARD + SUB + last * (rows - SUB), SUB)
            for level in range(levels):
                for tile in range(tiles):
                    lanes = pl.ds(tile * LANES, LANES)
                    u, v, w, p, t, s = (ext_ref[item, level, tile, here] for item in range(6))
                    out_ref[level, 0, :, lanes] = p
                    out_ref[level, 1, :, lanes] = v
                    for place, own, more in ((2, u, w), (3, t, s)):
                        more = pltpu.roll(more, 4, 0)
                        out_ref[level, place, :, lanes] = jnp.where(upper, own, more) if last else jnp.where(upper, more, own)

    for bottom in range(2):
        pl.when(facts[4] == bottom)(functools.partial(pack, bottom))


def nudge_kernel(facts, rate_ref, ext_ref, own_ref, far_ref, wide_ref, by_ref, out_ref, modes_ref, back_ref, done_ref, sem):
    fields, levels, rows, cols = out_ref.shape
    tiles = cols // LANES
    half = levels // 2
    pieces = 2 * own_ref.shape[0]
    chunk = own_ref.shape[2]
    mine = facts[2]
    for piece in range(pieces):
        target = pl.multiple_of(jnp.bitwise_xor(mine, piece) * chunk, SUB)
        source = own_ref if piece < pieces // 2 else far_ref
        modes_ref[:, pl.ds(target, chunk)] = source[piece % (pieces // 2)]
    lane = lax.broadcasted_iota(jnp.int32, (MODES, LANES), 1)
    lower = lax.broadcasted_iota(jnp.int32, (rows, LANES), 1) < MODES
    for field in range(fields):
        for pair in range(half):
            factor = jnp.where(lane < MODES, rate_ref[field, pair], rate_ref[field, pair + half])
            high, low = split(modes_ref[field, pair * MODES : (pair + 1) * MODES] * factor)
            out = dot(by_ref[...], jnp.concatenate([high, low], axis=1))
            out = out[:rows] + out[rows:]
            out = out[:, :LANES] + out[:, LANES:]
            high, low = split(out)
            high_turned, low_turned = split(pltpu.roll(out, MODES, 1))
            here = pl.ds(pair * rows, rows)
            back_ref[field, 0, here, :LANES] = jnp.where(lower, high, low_turned)
            back_ref[field, 1, here, :LANES] = jnp.where(lower, high_turned, low)
            for side in range(2):
                back_ref[field, side, here, LANES:] = high
    main = pl.ds(GUARD + SUB, rows)
    last_lane = lax.broadcasted_iota(jnp.int32, (rows, LANES), 1) == LANES - 1
    stores = []
    for field in range(fields):
        for level in range(levels):
            if level % half == 0:
                side = level // half
                tendency = dot(back_ref[field, side], wide_ref[side])
            first = (level % half) * rows
            for tile in range(tiles):
                lanes = pl.ds(tile * LANES, LANES)
                value = ext_ref[field, level, tile, main]
                if field == 0:
                    before = ext_ref[field, level, (tile - 1) % (tiles + 1), main]
                    value = pltpu.roll(jnp.where(last_lane, before, value), 1, 1)
                done_ref[field, level, :, lanes] = value - tendency[first : first + rows, lanes.start : lanes.start + LANES]
            if level % half == half - 1:
                part = pl.ds(level + 1 - half, half)
                place = sem.at[field, level // half]
                stores.append(pltpu.make_async_copy(done_ref.at[field, part], out_ref.at[field, part], place))
                stores[-1].start()
    for copy in stores:
        copy.wait()


def band_lanes(level_count):
    starts = lane_starts(level_count)
    for item in range(6):
        for level in range(level_count):
            yield item, level, REACH_X[item], GROUP_X[item], starts[item] + REACH_X[item] * level


def band_kernel(facts, _, a_ref, b_ref, bx_hbm, by_hbm, ext_ref, wide_ref, by_ref, *refs, rows, cols):
    *bands, sem = refs
    levels = ext_ref.shape[1]
    tiles = cols // LANES
    main = GUARD + SUB
    tables = [pltpu.make_async_copy(by_hbm.at[facts[1]], by_ref, sem.at[3, 0])]
    for side in range(2):
        for block, part in ((0, 0), (1, 0), (2 + side, 1)):
            target = wide_ref.at[side, pl.ds(block * MODES, MODES)]
            tables.append(pltpu.make_async_copy(bx_hbm.at[facts[0], part], target, sem.at[min(block, 2), side]))
    for copy in tables:
        copy.start()
    for side in range(2):
        wide_ref[side, (3 - side) * MODES : (4 - side) * MODES] = jnp.zeros((MODES, cols), wide_ref.dtype)
    zero = jnp.zeros((SUB, LANES), jnp.float32)
    for item in (1, 3):
        for level in range(levels):
            for tile in range(tiles + 1):
                ext_ref[item, level, tile, pl.ds(0, SUB)] = zero
                ext_ref[item, level, tile, pl.ds(main + rows + SUB, SUB)] = zero

    def place_slabs(odd):
        for phase, slab in enumerate((a_ref, b_ref)):
            base = GUARD if (odd == 1) == (phase == 0) else main + rows
            for item, place, turn in ((3, 0, 0), (1, 1, 0), (0, 2, 0), (2, 2, 4), (4, 3, 0), (5, 3, 4)):
                for level in range(levels):
                    for tile in range(tiles):
                        value = slab[level, place, :, tile * LANES : (tile + 1) * LANES]
                        if turn:
                            value = pltpu.roll(value, turn, 0)
                        ext_ref[item, level, tile, pl.ds(base, SUB)] = value

    for odd in range(2):
        pl.when(facts[6] == odd)(functools.partial(place_slabs, odd))
    lane = lax.broadcasted_iota(jnp.int32, (SUB, LANES), 1)

    def pack_band(band, right):
        parts = rows // SUB + 2
        packed = [[jnp.zeros((SUB, LANES), jnp.float32) for _ in range(2)] for _ in range(parts)]
        for item, level, width, group, first in band_lanes(levels):
            inside = (lane >= first) & (lane < first + width)
            for part in range(parts):
                tile = ext_ref[item, level, (tiles - 1) * right, pl.ds(part * SUB + GUARD, SUB)]
                moved = pltpu.roll(tile, (first + right * width) % LANES, 1)
                packed[part][group] = jnp.where(inside, moved, packed[part][group])
        for part in range(parts):
            for group in range(2):
                band[pl.ds(part * SUB, SUB), group * LANES : (group + 1) * LANES] = packed[part][group]

    for index, band in enumerate(bands):
        for right in range(2):
            pl.when((facts[3] ^ index) == right)(functools.partial(pack_band, band, right))
    for copy in tables:
        copy.wait()


def substep_kernel(facts, *refs, step, levels, rows, cols):
    bands, ext_ref = refs[1:-1], refs[-1]
    tiles = cols // LANES
    chunks = rows // SUB
    lane = lax.broadcasted_iota(jnp.int32, (SUB, LANES), 1)

    def unpack_bands(odd):
        for item, level, width, group, first in band_lanes(levels):
            for part in range(chunks + 2):
                value = jnp.zeros((SUB, LANES), jnp.float32)
                for phase, band in enumerate(bands):
                    left = odd if phase == 0 else 1 - odd
                    source = band[pl.ds(part * SUB, SUB), group * LANES : (group + 1) * LANES]
                    moved = pltpu.roll(source, (2 * LANES - first - left * width) % LANES, 1)
                    value = jnp.where(lane >= LANES - width if left else lane < width, moved, value)
                ext_ref[item, level, tiles, pl.ds(part * SUB + GUARD, SUB)] = value

    if step == 0:
        for odd in range(2):
            pl.when(facts[5] == odd)(functools.partial(unpack_bands, odd))

    quarter = 0.5 * COURANT
    sides = [jnp.where(facts[place] == 1, 1.0, 0.0) for place in (7, 8, 9, 10)]
    has_left, has_right, has_top, has_bottom = sides
    inner = jnp.where(lane == LANES - 1, has_right, 1.0)
    outer = jnp.where(lane < LANES // 2, has_right, jnp.where(lane == LANES - 1, 1.0, has_left))
    ring = tiles + 1

    def ahead(values, tile, count):
        moved = jnp.where(lane < count, values[(tile + 1) % ring], values[tile])
        return pltpu.roll(moved, LANES - count, 1)

    def behind(values, tile, count):
        moved = jnp.where(lane >= LANES - count, values[(tile - 1) % ring], values[tile])
        return pltpu.roll(moved, count, 1)

    u_ref, v_ref, w_ref, p_ref, t_ref, s_ref = (ext_ref.at[item] for item in range(6))
    first, last = step == 0, step == SUBSTEPS - 1

    def flush(pending):
        for ref, level, tile, here, value in pending:
            ref[level, tile, here] = value

    def winds(chunk, only_v=False):
        row = GUARD + chunk * SUB
        here = pl.ds(row, SUB)
        x_tiles = tiles if last else ring
        limit = {0: has_top, chunks + 1: has_bottom}.get(chunk)
        before = None
        line = None if only_v else [p_ref[0, tile, here] for tile in range(ring)]
        for level in range(levels):
            made = []
            for tile in range(x_tiles):
                slope = p_ref[level, tile, pl.ds(row + 1, SUB)] - p_ref[level, tile, pl.ds(row - 1, SUB)]
                if first:
                    slope = slope * (quarter if limit is None else quarter * limit)
                elif limit is not None:
                    slope = slope * limit
                made.append((v_ref, level, tile, here, v_ref[level, tile, here] - slope))
            if only_v:
                flush(made)
                continue
            old = [u_ref[level, tile, here] for tile in range(ring)]
            fresh = []
            for tile in range(ring):
                slope = ahead(line, tile, 2) - line[tile]
                edge = {tiles - 1: inner, tiles: outer}.get(tile)
                if first:
                    slope = slope * (quarter if edge is None else quarter * edge)
                elif edge is not None:
                    slope = slope * edge
                fresh.append(old[tile] - slope)
            for tile in range(ring):
                made.append((u_ref, level, tile, here, fresh[tile]))
            after = None
            if level + 1 < levels:
                after = [p_ref[level + 1, tile, here] for tile in range(ring)]
            for tile in range(x_tiles):
                if level == 0:
                    lift = after[tile]
                elif level == levels - 1:
                    lift = -before[tile]
                else:
                    lift = after[tile] - before[tile]
                warm = t_ref[level, tile, here]
                if first:
                    lift, warm = quarter * lift, COURANT * warm
                made.append((w_ref, level, tile, here, w_ref[level, tile, here] - (lift - warm)))
            before, line = line, after
            flush(made)

    def scalars(chunk):
        row = GUARD + chunk * SUB
        here = pl.ds(row, SUB)
        x_tiles = tiles if last else ring
        before, now = None, [w_ref[0, tile, here] for tile in range(x_tiles)]
        for level in range(levels):
            made = []
            line = [u_ref[level, tile, here] for tile in range(ring)]
            after = None
            if level + 1 < levels:
                after = [w_ref[level + 1, tile, here] for tile in range(x_tiles)]
            for tile in range(x_tiles):
                spread = line[tile] - behind(line, tile, 2)
                spread += v_ref[level, tile, pl.ds(row + 1, SUB)] - v_ref[level, tile, pl.ds(row - 1, SUB)]
                if level == 0:
                    spread += after[tile]
                elif level == levels - 1:
                    spread -= before[tile]
                else:
                    spread += after[tile] - before[tile]
                press, warm, speed = (ref[level, tile, here] for ref in (p_ref, t_ref, s_ref))
                if first:
                    press, warm, speed = quarter * press, COURANT * warm, (quarter * quarter) * speed
                    made.append((s_ref, level, tile, here, speed))
                press = press - speed * spread
                warm = warm - (COURANT * COURANT) * now[tile]
                if last:
                    press, warm = press * (1.0 / quarter), warm * (1.0 / COURANT)
                made.append((p_ref, level, tile, here, press))
                made.append((t_ref, level, tile, here, warm))
            before, now = now, after
            flush(made)

    def shift_rows(part, _):
        base = part * (chunks // 2 + 1) * SUB + GUARD
        for index in range(chunks // 2 + 1):
            here = pl.ds(pl.multiple_of(base + index * SUB, SUB), SUB)
            for level in range(levels):
                old = [u_ref[level, tile, here] for tile in range(ring)]
                for tile in range(ring):
                    u_ref[level, tile, here] = ahead(old, tile, 1)
        return 0

    if first:
        lax.fori_loop(0, 2, shift_rows, 0)
    if last:
        winds(0, True)
        winds(chunks + 1, True)
    span = range(1, chunks + 1) if last else range(chunks + 2)
    for chunk in span:
        winds(chunk)
    for chunk in span:
        scalars(chunk)


def solution(mesh):
    nx, ny = mesh.shape["gx"], mesh.shape["gy"]
    devices = nx * ny
    stages, middle = stages_of(devices)
    pieces = 1
    for stage in stages:
        pieces *= 1 << len(stage)
    pieces = max(pieces, 2)

    def decode(ref):
        number = ref[0]
        gx, gy = lax.div(number, ny), lax.rem(number, ny)
        mine = 0
        for stage in stages:
            for bit in reversed(stage):
                mine = mine * 2 + ((number >> bit) & 1)
        return (
            gx,
            gy,
            mine,
            (gx + 1) % 2,
            (gy + 1) % 2,
            gx % 2,
            gy % 2,
            jnp.where(gx > 0, 1, 0),
            jnp.where(gx < nx - 1, 1, 0),
            jnp.where(gy > 0, 1, 0),
            jnp.where(gy < ny - 1, 1, 0),
        )

    def informed(kernel, **static):
        def body(info, *refs):
            return kernel(decode(info), *refs, **static)

        return body

    x_phases = 1 if nx == 2 else 2

    def swap(value, mask):
        return lax.ppermute(value, ("gx", "gy"), [(i, i ^ mask) for i in range(devices)])

    def neighbours(value, axis, count, phase):
        pairs = []
        for low in range(phase, count - 1, 2):
            pairs += [(low, low + 1), (low + 1, low)]
        return lax.ppermute(value, axis, pairs)

    def on_device(state, driving, rate, sound_square):
        fields, levels, rows, cols = state.shape
        half = levels // 2
        chunk = half * MODES // pieces
        info = (lax.axis_index("gx") * ny + lax.axis_index("gy")).reshape(1)

        basis_x, weight_x = bases(MODES, cols * nx)
        basis_y, weight_y = bases(MODES, rows * ny)
        high, low = halves(weight_x)
        wx = np.concatenate([high, low], axis=0).T.reshape(nx, cols, 2 * MODES)
        high, low = halves(weight_y)
        wy = np.concatenate([high, low], axis=0).reshape(2 * MODES, ny, rows).transpose(1, 0, 2)
        high, low = halves(basis_x)
        bx = np.stack([high, low]).reshape(2, MODES, nx, cols).transpose(2, 0, 1, 3)
        high, low = halves(basis_y)
        by = np.stack([high, low]).reshape(2, MODES, ny, rows).transpose(2, 0, 3, 1).reshape(ny, 2 * rows, MODES)
        wx, wy, bx, by = (jnp.asarray(np.ascontiguousarray(t)) for t in (wx, wy, bx, by))

        hbm = pl.BlockSpec(memory_space=pltpu.HBM)
        vmem = pl.BlockSpec(memory_space=pltpu.VMEM)

        def call(kernel, name, shapes, ins, scratch, operands, flops=0, data=0, prefetch=1, aliases=None, limit=VMEM_LIMIT):
            return pl.pallas_call(
                kernel,
                grid_spec=pltpu.PrefetchScalarGridSpec(
                    num_scalar_prefetch=prefetch,
                    grid=(),
                    in_specs=ins,
                    out_specs=[vmem if name != "nudge" else hbm for _ in shapes],
                    scratch_shapes=scratch,
                ),
                out_shape=shapes,
                input_output_aliases=aliases or {},
                compiler_params=pltpu.CompilerParams(vmem_limit_bytes=limit),
                cost_estimate=pl.CostEstimate(flops=flops, bytes_accessed=data, transcendentals=0),
            )(*operands)

        def array(shape, dtype=jnp.float32):
            return jax.ShapeDtypeStruct(shape, dtype)

        tiles = cols // LANES
        slab_shape = (levels, 4, SUB, cols)
        piece_shape = (pieces // 2, fields, chunk, LANES)
        ext_shape = (6, levels, tiles + 1, rows + 2 * SUB + 2 * GUARD, LANES)
        band_shape = (rows + 2 * SUB, 2 * LANES)
        ext, slab_a, slab_b, keep, send = call(
            informed(head_kernel),
            "head",
            [array(ext_shape), *[array(slab_shape)] * 2, *[array(piece_shape)] * 2],
            [hbm] * 5,
            [
                pltpu.VMEM((fields, levels, rows, cols), jnp.float32),
                pltpu.VMEM((cols, 2 * MODES), jnp.bfloat16),
                pltpu.VMEM((2 * MODES, rows), jnp.bfloat16),
                pltpu.VMEM((fields, half * rows, 2 * LANES), jnp.bfloat16),
                pltpu.VMEM((fields, half * MODES, LANES), jnp.float32),
                pltpu.SemaphoreType.DMA((fields + 2, tiles + 1)),
            ],
            (info, *(pltpu.with_memory_space_constraint(x, pltpu.HBM) for x in (state, driving, sound_square, wx, wy))),
            600_000_000,
            9_000_000,
        )
        slab_a = neighbours(slab_a, "gy", ny, 0)
        slab_b = neighbours(slab_b, "gy", ny, 1)

        ext, wide, back, *bands = call(
            informed(band_kernel, rows=rows, cols=cols),
            "band",
            [
                array(ext_shape),
                array((2, 4 * MODES, cols), jnp.bfloat16),
                array((2 * rows, MODES), jnp.bfloat16),
            ]
            + [array(band_shape)] * x_phases,
            [vmem, vmem, vmem, hbm, hbm],
            [pltpu.SemaphoreType.DMA((4, 2))],
            (info, ext, slab_a, slab_b, bx, by),
            1_000_000,
            10_000_000,
            aliases={1: 0},
        )
        bands = [neighbours(band, "gx", nx, index) for index, band in enumerate(bands)]

        for step in range(SUBSTEPS):
            extra = bands if step == 0 else []
            (ext,) = call(
                informed(substep_kernel, step=step, levels=levels, rows=rows, cols=cols),
                f"substep_{step}",
                [array(ext_shape)],
                [vmem] * (1 + len(extra)),
                [],
                (info, ext, *extra),
                10_000_000,
                8_000_000,
                aliases={1: 0},
            )

        value = None
        for place, stage in enumerate(stages):
            masks = masks_of(stage)
            if place == 0:
                value = keep + swap(send, masks[1])
                continue
            value = value.reshape((len(masks), value.shape[0] // len(masks)) + value.shape[1:])
            moved = [swap(value[i], masks[i]) for i in range(1, len(masks))]
            value = functools.reduce(jnp.add, moved, value[0])
        moved = [swap(value, mask) for i, mask in enumerate(masks_of(middle)) if i]
        value = functools.reduce(jnp.add, moved, value)
        for place in reversed(range(1, len(stages))):
            moved = [swap(value, mask) for i, mask in enumerate(masks_of(stages[place])) if i]
            value = jnp.concatenate([value] + moved, axis=0)
        far = swap(value, masks_of(stages[0])[1])

        (out,) = call(
            informed(nudge_kernel),
            "nudge",
            [array(state.shape)],
            [vmem] * 5,
            [
                pltpu.VMEM((fields, half * MODES, LANES), jnp.float32),
                pltpu.VMEM((fields, 2, half * rows, 2 * LANES), jnp.bfloat16),
                pltpu.VMEM((fields, levels, rows, cols), jnp.float32),
                pltpu.SemaphoreType.DMA((fields, 2)),
            ],
            (info, rate, ext, value, far, wide, back),
            600_000_000,
            8_500_000,
            prefetch=2,
        )
        return out

    return jax.shard_map(
        on_device,
        mesh=mesh,
        in_specs=(P(None, None, "gy", "gx"), P(None, None, "gy", "gx"), P(), P(None, "gy", "gx")),
        out_specs=P(None, None, "gy", "gx"),
        check_vma=False,
    )
```

```python
import functools

import jax
import jax.numpy as jnp
import numpy as np
from jax import lax
from jax.experimental import pallas as pl
from jax.experimental.pallas import tpu as pltpu
from jax.sharding import PartitionSpec as P


MODES = 64
SUBSTEPS = 3
COURANT = 0.5
LANES = 128
SUB = 8
GUARD = 8
VMEM_LIMIT = 32 << 20

REACH_X = (5, 4, 4, 6, 4, 4)
GROUP_X = (0, 0, 1, 0, 1, 1)


def lane_starts(levels):
    used = [0, 0]
    starts = []
    for width, group in zip(REACH_X, GROUP_X):
        starts.append(used[group])
        used[group] += width * levels
    assert max(used) <= LANES
    return starts


def bases(count, total):
    index = np.arange(total, dtype=np.int64)
    order = np.arange(count, dtype=np.int64)
    freq = np.where(order < count // 2, order, order - count // 2 + 1)
    wrapped = (freq[:, None] * (2 * index[None, :] + 1)) % (2 * total)
    phase = np.pi * wrapped.astype(np.float64) / total
    basis = np.where(order[:, None] < count // 2, np.cos(phase), np.sin(phase))
    scaling = np.where(order == 0, 1.0 / total, 2.0 / total)
    basis32 = basis.astype(np.float32)
    weight32 = (basis * scaling[:, None]).astype(np.float32)
    return basis32, weight32


def halves(table):
    high = table.astype(jnp.bfloat16)
    low = (table - high.astype(np.float32)).astype(jnp.bfloat16)
    return np.asarray(high), np.asarray(low)


def split(value):
    high = value.astype(jnp.bfloat16)
    low = (value - high.astype(jnp.float32)).astype(jnp.bfloat16)
    return high, low


def dot(left, right):
    return jnp.dot(left, right, preferred_element_type=jnp.float32)


def masks_of(bits):
    masks = [0]
    for bit in bits:
        masks = masks + [mask | (1 << bit) for mask in masks]
    return masks


def stages_of(devices):
    total = devices.bit_length() - 1
    assert devices == 1 << total
    left = list(range(total))
    stages = []
    if left:
        stages.append([left.pop(0)])
    while len(left) > 3 and len(stages) < 3:
        stages.append([left.pop(0), left.pop()])
    return stages, left


def head_kernel(
    facts,
    state_ref,
    driving_ref,
    sound_ref,
    wx_hbm,
    wy_hbm,
    ext_ref,
    a_ref,
    b_ref,
    keep_ref,
    send_ref,
    other_ref,
    wx_ref,
    wy_ref,
    packed_ref,
    modes_ref,
    sem,
):
    fields, levels, rows, cols = state_ref.shape
    tiles = cols // LANES
    half = levels // 2
    pieces = 2 * keep_ref.shape[0]
    chunk = keep_ref.shape[2]
    main = pl.ds(GUARD + SUB, rows)

    def fetch(item):
        source = state_ref.at[item] if item < fields else sound_ref
        copies = [
            pltpu.make_async_copy(
                source.at[:, :, pl.ds(tile * LANES, LANES)], ext_ref.at[item, :, tile, main], sem.at[item, tile]
            )
            for tile in range(tiles)
        ]
        if item < fields:
            copies.append(pltpu.make_async_copy(driving_ref.at[item], other_ref.at[item], sem.at[item, tiles]))
        return copies

    tables = [
        pltpu.make_async_copy(wx_hbm.at[facts[0]], wx_ref, sem.at[fields + 1, 0]),
        pltpu.make_async_copy(wy_hbm.at[facts[1]], wy_ref, sem.at[fields + 1, 1]),
    ]
    loads = [fetch(item) for item in range(fields + 1)]
    for copy in [*tables, *(copy for load in loads for copy in load)]:
        copy.start()
    lane = lax.broadcasted_iota(jnp.int32, (half * rows, LANES), 1)
    for copy in tables:
        copy.wait()
    weights = wx_ref[...]

    def rows_of(field):
        for pair in range(half):
            out = dot(wy_ref[...], packed_ref[field, pair * rows : (pair + 1) * rows])
            out = out[:MODES] + out[MODES:]
            modes_ref[field, pair * MODES : (pair + 1) * MODES] = out[:, :LANES] + out[:, LANES:]

    for field in range(fields):
        for copy in loads[field]:
            copy.wait()
        sides = []
        for side in range(2):
            part = pl.ds(side * half, half)
            tile_of = [ext_ref[field, part, tile, main].reshape(half * rows, LANES) for tile in range(tiles)]
            diff = jnp.concatenate(tile_of, axis=1) - other_ref[field, part].reshape(half * rows, cols)
            high, low = split(diff)
            both = dot(high, weights) + dot(low, weights)
            sides.append(both + pltpu.roll(both, MODES, 1))
        high, low = split(jnp.where(lane < MODES, sides[0], sides[1]))
        packed_ref[field, :, :LANES] = high
        packed_ref[field, :, LANES:] = low
        if field:
            rows_of(field - 1)
    for copy in loads[fields]:
        copy.wait()
    rows_of(fields - 1)
    mine = facts[2]
    for piece in range(pieces):
        source = pl.multiple_of(jnp.bitwise_xor(mine, piece) * chunk, SUB)
        target = keep_ref if piece < pieces // 2 else send_ref
        target[piece % (pieces // 2)] = modes_ref[:, pl.ds(source, chunk)]

    upper = lax.broadcasted_iota(jnp.int32, (SUB, LANES), 0) >= 4

    def pack(bottom):
        for out_ref, last in ((a_ref, bottom), (b_ref, 1 - bottom)):
            here = pl.ds(GUARD + SUB + last * (rows - SUB), SUB)
            for level in range(levels):
                for tile in range(tiles):
                    lanes = pl.ds(tile * LANES, LANES)
                    u, v, w, p, t, s = (ext_ref[item, level, tile, here] for item in range(6))
                    out_ref[level, 0, :, lanes] = p
                    out_ref[level, 1, :, lanes] = v
                    for place, own, more in ((2, u, w), (3, t, s)):
                        more = pltpu.roll(more, 4, 0)
                        out_ref[level, place, :, lanes] = jnp.where(upper, own, more) if last else jnp.where(upper, more, own)

    for bottom in range(2):
        pl.when(facts[4] == bottom)(functools.partial(pack, bottom))


def nudge_kernel(facts, rate_ref, ext_ref, own_ref, far_ref, wide_ref, by_ref, out_ref, modes_ref, back_ref, done_ref, sem):
    fields, levels, rows, cols = out_ref.shape
    tiles = cols // LANES
    half = levels // 2
    pieces = 2 * own_ref.shape[0]
    chunk = own_ref.shape[2]
    mine = facts[2]
    for piece in range(pieces):
        target = pl.multiple_of(jnp.bitwise_xor(mine, piece) * chunk, SUB)
        source = own_ref if piece < pieces // 2 else far_ref
        modes_ref[:, pl.ds(target, chunk)] = source[piece % (pieces // 2)]
    lane = lax.broadcasted_iota(jnp.int32, (MODES, LANES), 1)
    lower = lax.broadcasted_iota(jnp.int32, (rows, LANES), 1) < MODES
    main = pl.ds(GUARD + SUB, rows)
    last_lane = lax.broadcasted_iota(jnp.int32, (rows, LANES), 1) == LANES - 1

    def back(field):
        for pair in range(half):
            factor = jnp.where(lane < MODES, rate_ref[field, pair], rate_ref[field, pair + half])
            high, low = split(modes_ref[field, pair * MODES : (pair + 1) * MODES] * factor)
            out = dot(by_ref[...], jnp.concatenate([high, low], axis=1))
            out = out[:rows] + out[rows:]
            out = out[:, :LANES] + out[:, LANES:]
            high, low = split(out)
            high_turned, low_turned = split(pltpu.roll(out, MODES, 1))
            here = pl.ds(pair * rows, rows)
            back_ref[field, 0, here, :LANES] = jnp.where(lower, high, low_turned)
            back_ref[field, 1, here, :LANES] = jnp.where(lower, high_turned, low)
            for side in range(2):
                back_ref[field, side, here, LANES:] = high

    back(0)
    stores = []
    for field in range(fields):
        if field + 1 < fields:
            back(field + 1)
        for level in range(levels):
            if level % half == 0:
                side = level // half
                tendency = dot(back_ref[field, side], wide_ref[side])
            first = (level % half) * rows
            for tile in range(tiles):
                lanes = pl.ds(tile * LANES, LANES)
                value = ext_ref[field, level, tile, main]
                if field == 0:
                    before = ext_ref[field, level, (tile - 1) % (tiles + 1), main]
                    value = pltpu.roll(jnp.where(last_lane, before, value), 1, 1)
                done_ref[field, level, :, lanes] = value - tendency[first : first + rows, lanes.start : lanes.start + LANES]
            if level % half == half - 1:
                part = pl.ds(level + 1 - half, half)
                place = sem.at[field, level // half]
                stores.append(pltpu.make_async_copy(done_ref.at[field, part], out_ref.at[field, part], place))
                stores[-1].start()
    for copy in stores:
        copy.wait()


def band_lanes(level_count):
    starts = lane_starts(level_count)
    for item in range(6):
        for level in range(level_count):
            yield item, level, REACH_X[item], GROUP_X[item], starts[item] + REACH_X[item] * level


def pack_bands(facts, bands, ext_ref, parts, tiles):
    levels = ext_ref.shape[1]
    lane = lax.broadcasted_iota(jnp.int32, (SUB, LANES), 1)

    def pack(band, right):
        packed = [[jnp.zeros((SUB, LANES), jnp.float32) for _ in range(2)] for _ in parts]
        for item, level, width, group, first in band_lanes(levels):
            inside = (lane >= first) & (lane < first + width)
            for place, part in enumerate(parts):
                tile = ext_ref[item, level, (tiles - 1) * right, pl.ds(part * SUB + GUARD, SUB)]
                moved = pltpu.roll(tile, (first + right * width) % LANES, 1)
                packed[place][group] = jnp.where(inside, moved, packed[place][group])
        for place, part in enumerate(parts):
            for group in range(2):
                band[pl.ds(part * SUB, SUB), group * LANES : (group + 1) * LANES] = packed[place][group]

    for index, band in enumerate(bands):
        for right in range(2):
            pl.when((facts[3] ^ index) == right)(functools.partial(pack, band, right))


def shift_down(ext_ref, parts, tiles):
    lane = lax.broadcasted_iota(jnp.int32, (SUB, LANES), 1)
    for part in parts:
        here = pl.ds(part * SUB + GUARD, SUB)
        for level in range(ext_ref.shape[1]):
            old = [ext_ref[0, level, tile, here] for tile in range(tiles)]
            old += [old[0], old[0]]
            for tile in range(tiles + 1):
                value = old[tile] if tile >= tiles - 1 else jnp.where(lane == 0, old[tile + 1], old[tile])
                ext_ref[0, level, tile, here] = pltpu.roll(value, LANES - 1, 1)


def prepare_kernel(facts, _, bx_hbm, by_hbm, ext_ref, wide_ref, by_ref, *refs, rows, cols):
    *bands, sem = refs
    levels = ext_ref.shape[1]
    tiles = cols // LANES
    tables = [pltpu.make_async_copy(by_hbm.at[facts[1]], by_ref, sem.at[3, 0])]
    for side in range(2):
        for block, part in ((0, 0), (1, 0), (2 + side, 1)):
            target = wide_ref.at[side, pl.ds(block * MODES, MODES)]
            tables.append(pltpu.make_async_copy(bx_hbm.at[facts[0], part], target, sem.at[min(block, 2), side]))
    for copy in tables:
        copy.start()
    for side in range(2):
        wide_ref[side, (3 - side) * MODES : (4 - side) * MODES] = jnp.zeros((MODES, cols), wide_ref.dtype)
    zero = jnp.zeros((SUB, LANES), jnp.float32)
    for item in (1, 3):
        for level in range(levels):
            for tile in range(tiles + 1):
                ext_ref[item, level, tile, pl.ds(0, SUB)] = zero
                ext_ref[item, level, tile, pl.ds(GUARD + 2 * SUB + rows, SUB)] = zero
    parts = range(1, rows // SUB + 1)
    pack_bands(facts, bands, ext_ref, parts, tiles)
    shift_down(ext_ref, parts, tiles)
    for copy in tables:
        copy.wait()


def band_kernel(facts, *refs, x_phases, slabs, rows, cols):
    a_ref, b_refs = refs[1 + x_phases], refs[2 + x_phases : 2 + x_phases + slabs]
    ext_ref, *bands = refs[2 + x_phases + slabs :]
    levels = ext_ref.shape[1]
    tiles = cols // LANES

    def place_slabs(odd):
        for phase, sources in enumerate(((a_ref,), b_refs)):
            base = GUARD if (odd == 1) == (phase == 0) else GUARD + SUB + rows
            for item, place, turn in ((3, 0, 0), (1, 1, 0), (0, 2, 0), (2, 2, 4), (4, 3, 0), (5, 3, 4)):
                for level in range(levels):
                    for tile in range(tiles):
                        lanes = slice(tile * LANES, (tile + 1) * LANES)
                        value = functools.reduce(jnp.add, [ref[level, place, :, lanes] for ref in sources])
                        if turn:
                            value = pltpu.roll(value, turn, 0)
                        ext_ref[item, level, tile, pl.ds(base, SUB)] = value

    for odd in range(2):
        pl.when(facts[6] == odd)(functools.partial(place_slabs, odd))
    parts = (0, rows // SUB + 1)
    pack_bands(facts, bands, ext_ref, parts, tiles)
    shift_down(ext_ref, parts, tiles)


def substep_kernel(facts, *refs, step, levels, rows, cols):
    bands, ext_ref = refs[1:-1], refs[-1]
    tiles = cols // LANES
    chunks = rows // SUB
    lane = lax.broadcasted_iota(jnp.int32, (SUB, LANES), 1)

    def unpack_bands(odd):
        for item, level, width, group, first in band_lanes(levels):
            down = 1 if item == 0 else 0
            for part in range(chunks + 2):
                here = pl.ds(part * SUB + GUARD, SUB)
                value = edge = jnp.zeros((SUB, LANES), jnp.float32)
                if down:
                    value = jnp.where(lane == LANES - 1, ext_ref[0, level, tiles, here], value)
                for phase, band in enumerate(bands):
                    left = odd if phase == 0 else 1 - odd
                    source = band[pl.ds(part * SUB, SUB), group * LANES : (group + 1) * LANES]
                    moved = pltpu.roll(source, (2 * LANES - first - left * width - down) % LANES, 1)
                    if left:
                        inside = (lane >= LANES - width - down) & (lane < LANES - down)
                    else:
                        inside = lane < width - down
                        edge = moved
                    value = jnp.where(inside, moved, value)
                ext_ref[item, level, tiles, here] = value
                if down:
                    old = ext_ref[0, level, tiles - 1, here]
                    ext_ref[0, level, tiles - 1, here] = jnp.where(lane == LANES - 1, edge, old)

    if step == 0:
        for odd in range(2):
            pl.when(facts[5] == odd)(functools.partial(unpack_bands, odd))

    quarter = 0.5 * COURANT
    sides = [jnp.where(facts[place] == 1, 1.0, 0.0) for place in (7, 8, 9, 10)]
    has_left, has_right, has_top, has_bottom = sides
    inner = jnp.where(lane == LANES - 1, has_right, 1.0)
    outer = jnp.where(lane < LANES // 2, has_right, jnp.where(lane == LANES - 1, 1.0, has_left))
    ring = tiles + 1

    def ahead(values, tile, count):
        moved = jnp.where(lane < count, values[(tile + 1) % ring], values[tile])
        return pltpu.roll(moved, LANES - count, 1)

    def behind(values, tile, count):
        moved = jnp.where(lane >= LANES - count, values[(tile - 1) % ring], values[tile])
        return pltpu.roll(moved, count, 1)

    u_ref, v_ref, w_ref, p_ref, t_ref, s_ref = (ext_ref.at[item] for item in range(6))
    first, last = step == 0, step == SUBSTEPS - 1

    def flush(pending):
        for ref, level, tile, here, value in pending:
            ref[level, tile, here] = value

    def winds(chunk, only_v=False):
        row = GUARD + chunk * SUB
        here = pl.ds(row, SUB)
        x_tiles = tiles if last else ring
        limit = {0: has_top, chunks + 1: has_bottom}.get(chunk)
        before = None
        line = None if only_v else [p_ref[0, tile, here] for tile in range(ring)]
        for level in range(levels):
            made = []
            for tile in range(x_tiles):
                slope = p_ref[level, tile, pl.ds(row + 1, SUB)] - p_ref[level, tile, pl.ds(row - 1, SUB)]
                if first:
                    slope = slope * (quarter if limit is None else quarter * limit)
                elif limit is not None:
                    slope = slope * limit
                made.append((v_ref, level, tile, here, v_ref[level, tile, here] - slope))
            if only_v:
                flush(made)
                continue
            old = [u_ref[level, tile, here] for tile in range(ring)]
            fresh = []
            for tile in range(ring):
                slope = ahead(line, tile, 2) - line[tile]
                edge = {tiles - 1: inner, tiles: outer}.get(tile)
                if first:
                    slope = slope * (quarter if edge is None else quarter * edge)
                elif edge is not None:
                    slope = slope * edge
                fresh.append(old[tile] - slope)
            for tile in range(ring):
                made.append((u_ref, level, tile, here, fresh[tile]))
            after = None
            if level + 1 < levels:
                after = [p_ref[level + 1, tile, here] for tile in range(ring)]
            for tile in range(x_tiles):
                if level == 0:
                    lift = after[tile]
                elif level == levels - 1:
                    lift = -before[tile]
                else:
                    lift = after[tile] - before[tile]
                warm = t_ref[level, tile, here]
                if first:
                    lift, warm = quarter * lift, COURANT * warm
                made.append((w_ref, level, tile, here, w_ref[level, tile, here] - (lift - warm)))
            before, line = line, after
            flush(made)

    def scalars(chunk):
        row = GUARD + chunk * SUB
        here = pl.ds(row, SUB)
        x_tiles = tiles if last else ring
        before, now = None, [w_ref[0, tile, here] for tile in range(x_tiles)]
        for level in range(levels):
            made = []
            line = [u_ref[level, tile, here] for tile in range(ring)]
            after = None
            if level + 1 < levels:
                after = [w_ref[level + 1, tile, here] for tile in range(x_tiles)]
            for tile in range(x_tiles):
                spread = line[tile] - behind(line, tile, 2)
                spread += v_ref[level, tile, pl.ds(row + 1, SUB)] - v_ref[level, tile, pl.ds(row - 1, SUB)]
                if level == 0:
                    spread += after[tile]
                elif level == levels - 1:
                    spread -= before[tile]
                else:
                    spread += after[tile] - before[tile]
                press, warm, speed = (ref[level, tile, here] for ref in (p_ref, t_ref, s_ref))
                if first:
                    press, warm, speed = quarter * press, COURANT * warm, (quarter * quarter) * speed
                    made.append((s_ref, level, tile, here, speed))
                press = press - speed * spread
                warm = warm - (COURANT * COURANT) * now[tile]
                if last:
                    press, warm = press * (1.0 / quarter), warm * (1.0 / COURANT)
                made.append((p_ref, level, tile, here, press))
                made.append((t_ref, level, tile, here, warm))
            before, now = now, after
            flush(made)

    if last:
        winds(0, True)
        winds(chunks + 1, True)
    span = range(1, chunks + 1) if last else range(chunks + 2)
    for chunk in span:
        winds(chunk)
    for chunk in span:
        scalars(chunk)


def solution(mesh):
    nx, ny = mesh.shape["gx"], mesh.shape["gy"]
    devices = nx * ny
    stages, middle = stages_of(devices)
    pieces = 1
    for stage in stages:
        pieces *= 1 << len(stage)
    pieces = max(pieces, 2)

    def decode(ref):
        number = ref[0]
        gx, gy = lax.div(number, ny), lax.rem(number, ny)
        mine = 0
        for stage in stages:
            for bit in reversed(stage):
                mine = mine * 2 + ((number >> bit) & 1)
        return (
            gx,
            gy,
            mine,
            (gx + 1) % 2,
            (gy + 1) % 2,
            gx % 2,
            gy % 2,
            jnp.where(gx > 0, 1, 0),
            jnp.where(gx < nx - 1, 1, 0),
            jnp.where(gy > 0, 1, 0),
            jnp.where(gy < ny - 1, 1, 0),
        )

    def informed(kernel, **static):
        def body(info, *refs):
            return kernel(decode(info), *refs, **static)

        return body

    x_phases = 1 if nx == 2 else 2

    def swap(value, mask):
        return lax.ppermute(value, ("gx", "gy"), [(i, i ^ mask) for i in range(devices)])

    def neighbours(value, axis, count, phase, far=None):
        pairs = []
        for low in range(phase, count - 1, 2):
            if far is None or ((low + 1) % 4 == 0) == far:
                pairs += [(low, low + 1), (low + 1, low)]
        return lax.ppermute(value, axis, pairs)

    def on_device(state, driving, rate, sound_square):
        fields, levels, rows, cols = state.shape
        half = levels // 2
        chunk = half * MODES // pieces
        info = (lax.axis_index("gx") * ny + lax.axis_index("gy")).reshape(1)

        basis_x, weight_x = bases(MODES, cols * nx)
        basis_y, weight_y = bases(MODES, rows * ny)
        high, low = halves(weight_x)
        wx = np.concatenate([high, low], axis=0).T.reshape(nx, cols, 2 * MODES)
        high, low = halves(weight_y)
        wy = np.concatenate([high, low], axis=0).reshape(2 * MODES, ny, rows).transpose(1, 0, 2)
        high, low = halves(basis_x)
        bx = np.stack([high, low]).reshape(2, MODES, nx, cols).transpose(2, 0, 1, 3)
        high, low = halves(basis_y)
        by = np.stack([high, low]).reshape(2, MODES, ny, rows).transpose(2, 0, 3, 1).reshape(ny, 2 * rows, MODES)
        wx, wy, bx, by = (jnp.asarray(np.ascontiguousarray(t)) for t in (wx, wy, bx, by))

        hbm = pl.BlockSpec(memory_space=pltpu.HBM)
        vmem = pl.BlockSpec(memory_space=pltpu.VMEM)

        def call(kernel, name, shapes, ins, scratch, operands, flops=0, data=0, prefetch=1, aliases=None, limit=VMEM_LIMIT):
            return pl.pallas_call(
                kernel,
                grid_spec=pltpu.PrefetchScalarGridSpec(
                    num_scalar_prefetch=prefetch,
                    grid=(),
                    in_specs=ins,
                    out_specs=[vmem if name != "nudge" else hbm for _ in shapes],
                    scratch_shapes=scratch,
                ),
                out_shape=shapes,
                input_output_aliases=aliases or {},
                compiler_params=pltpu.CompilerParams(vmem_limit_bytes=limit),
                cost_estimate=pl.CostEstimate(flops=flops, bytes_accessed=data, transcendentals=0),
            )(*operands)

        def array(shape, dtype=jnp.float32):
            return jax.ShapeDtypeStruct(shape, dtype)

        tiles = cols // LANES
        slab_shape = (levels, 4, SUB, cols)
        piece_shape = (pieces // 2, fields, chunk, LANES)
        ext_shape = (6, levels, tiles + 1, rows + 2 * SUB + 2 * GUARD, LANES)
        band_shape = (rows + 2 * SUB, 2 * LANES)
        ext, slab_a, slab_b, keep, send = call(
            informed(head_kernel),
            "head",
            [array(ext_shape), *[array(slab_shape)] * 2, *[array(piece_shape)] * 2],
            [hbm] * 5,
            [
                pltpu.VMEM((fields, levels, rows, cols), jnp.float32),
                pltpu.VMEM((cols, 2 * MODES), jnp.bfloat16),
                pltpu.VMEM((2 * MODES, rows), jnp.bfloat16),
                pltpu.VMEM((fields, half * rows, 2 * LANES), jnp.bfloat16),
                pltpu.VMEM((fields, half * MODES, LANES), jnp.float32),
                pltpu.SemaphoreType.DMA((fields + 2, tiles + 1)),
            ],
            (info, *(pltpu.with_memory_space_constraint(x, pltpu.HBM) for x in (state, driving, sound_square, wx, wy))),
            600_000_000,
            9_000_000,
        )
        slab_a = neighbours(slab_a, "gy", ny, 0)
        slabs_b = [
            neighbours(slab_b, "gy", ny, 1, far)
            for far in (True, False)
            if any(((low + 1) % 4 == 0) == far for low in range(1, ny - 1, 2))
        ]

        ext, wide, back, *bands = call(
            informed(prepare_kernel, rows=rows, cols=cols),
            "prepare",
            [array(ext_shape), array((2, 4 * MODES, cols), jnp.bfloat16), array((2 * rows, MODES), jnp.bfloat16)]
            + [array(band_shape)] * x_phases,
            [vmem, hbm, hbm],
            [pltpu.SemaphoreType.DMA((4, 2))],
            (info, ext, bx, by),
            1_000_000,
            5_000_000,
            aliases={1: 0},
        )
        ext, *bands = call(
            informed(band_kernel, x_phases=x_phases, slabs=len(slabs_b), rows=rows, cols=cols),
            "band",
            [array(ext_shape)] + [array(band_shape)] * x_phases,
            [vmem] * (2 + x_phases + len(slabs_b)),
            [],
            (info, ext, *bands, slab_a, *slabs_b),
            1_000_000,
            5_000_000,
            aliases={1 + index: index for index in range(1 + x_phases)},
        )
        bands = [neighbours(band, "gx", nx, index) for index, band in enumerate(bands)]

        for step in range(SUBSTEPS):
            extra = bands if step == 0 else []
            (ext,) = call(
                informed(substep_kernel, step=step, levels=levels, rows=rows, cols=cols),
                f"substep_{step}",
                [array(ext_shape)],
                [vmem] * (1 + len(extra)),
                [],
                (info, ext, *extra),
                10_000_000,
                8_000_000,
                aliases={1: 0},
            )

        value = None
        for place, stage in enumerate(stages):
            masks = masks_of(stage)
            if place == 0:
                value = keep + swap(send, masks[1])
                continue
            value = value.reshape((len(masks), value.shape[0] // len(masks)) + value.shape[1:])
            moved = [swap(value[i], masks[i]) for i in range(1, len(masks))]
            value = functools.reduce(jnp.add, moved, value[0])
        moved = [swap(value, mask) for i, mask in enumerate(masks_of(middle)) if i]
        value = functools.reduce(jnp.add, moved, value)
        for place in reversed(range(1, len(stages))):
            moved = [swap(value, mask) for i, mask in enumerate(masks_of(stages[place])) if i]
            value = jnp.concatenate([value] + moved, axis=0)
        far = swap(value, masks_of(stages[0])[1])

        (out,) = call(
            informed(nudge_kernel),
            "nudge",
            [array(state.shape)],
            [vmem] * 5,
            [
                pltpu.VMEM((fields, half * MODES, LANES), jnp.float32),
                pltpu.VMEM((fields, 2, half * rows, 2 * LANES), jnp.bfloat16),
                pltpu.VMEM((fields, levels, rows, cols), jnp.float32),
                pltpu.SemaphoreType.DMA((fields, 2)),
            ],
            (info, rate, ext, value, far, wide, back),
            600_000_000,
            8_500_000,
            prefetch=2,
        )
        return out

    return jax.shard_map(
        on_device,
        mesh=mesh,
        in_specs=(P(None, None, "gy", "gx"), P(None, None, "gy", "gx"), P(), P(None, "gy", "gx")),
        out_specs=P(None, None, "gy", "gx"),
        check_vma=False,
    )
```

```python
import functools

import jax
import jax.numpy as jnp
import numpy as np
from jax import lax
from jax.experimental import pallas as pl
from jax.experimental.pallas import tpu as pltpu
from jax.sharding import PartitionSpec as P


MODES = 64
SUBSTEPS = 3
COURANT = 0.5
LANES = 128
SUB = 8
GUARD = 8
VMEM_LIMIT = 32 << 20

REACH_X = (5, 4, 4, 6, 4, 4)
GROUP_X = (0, 0, 1, 0, 1, 1)


def lane_starts(levels):
    used = [0, 0]
    starts = []
    for width, group in zip(REACH_X, GROUP_X):
        starts.append(used[group])
        used[group] += width * levels
    assert max(used) <= LANES
    return starts


def bases(count, total):
    index = np.arange(total, dtype=np.int64)
    order = np.arange(count, dtype=np.int64)
    freq = np.where(order < count // 2, order, order - count // 2 + 1)
    wrapped = (freq[:, None] * (2 * index[None, :] + 1)) % (2 * total)
    phase = np.pi * wrapped.astype(np.float64) / total
    basis = np.where(order[:, None] < count // 2, np.cos(phase), np.sin(phase))
    scaling = np.where(order == 0, 1.0 / total, 2.0 / total)
    basis32 = basis.astype(np.float32)
    weight32 = (basis * scaling[:, None]).astype(np.float32)
    return basis32, weight32


def halves(table):
    high = table.astype(jnp.bfloat16)
    low = (table - high.astype(np.float32)).astype(jnp.bfloat16)
    return np.asarray(high), np.asarray(low)


def split(value):
    high = value.astype(jnp.bfloat16)
    low = (value - high.astype(jnp.float32)).astype(jnp.bfloat16)
    return high, low


def dot(left, right):
    return jnp.dot(left, right, preferred_element_type=jnp.float32)


def masks_of(bits):
    masks = [0]
    for bit in bits:
        masks = masks + [mask | (1 << bit) for mask in masks]
    return masks


def stages_of(devices):
    total = devices.bit_length() - 1
    assert devices == 1 << total
    left = list(range(total))
    stages = []
    if left:
        stages.append([left.pop(0)])
    while len(left) > 3 and len(stages) < 3:
        stages.append([left.pop(0), left.pop()])
    return stages, left


def head_kernel(
    facts,
    state_ref,
    driving_ref,
    sound_ref,
    wx_hbm,
    wy_hbm,
    ext_ref,
    a_ref,
    b_ref,
    keep_ref,
    send_ref,
    other_ref,
    wx_ref,
    wy_ref,
    packed_ref,
    modes_ref,
    sem,
):
    fields, levels, rows, cols = state_ref.shape
    tiles = cols // LANES
    half = levels // 2
    pieces = 2 * keep_ref.shape[0]
    chunk = keep_ref.shape[2]
    main = pl.ds(GUARD + SUB, rows)

    def fetch(item):
        source = state_ref.at[item] if item < fields else sound_ref
        copies = [
            pltpu.make_async_copy(
                source.at[:, :, pl.ds(tile * LANES, LANES)], ext_ref.at[item, :, tile, main], sem.at[item, tile]
            )
            for tile in range(tiles)
        ]
        if item < fields:
            copies.append(pltpu.make_async_copy(driving_ref.at[item], other_ref.at[item], sem.at[item, tiles]))
        return copies

    tables = [
        pltpu.make_async_copy(wx_hbm.at[facts[0]], wx_ref, sem.at[fields + 1, 0]),
        pltpu.make_async_copy(wy_hbm.at[facts[1]], wy_ref, sem.at[fields + 1, 1]),
    ]
    loads = [fetch(item) for item in range(fields + 1)]
    for copy in [*tables, *(copy for load in loads for copy in load)]:
        copy.start()
    lane = lax.broadcasted_iota(jnp.int32, (half * rows, LANES), 1)
    for copy in tables:
        copy.wait()
    weights = wx_ref[...]

    def rows_of(field):
        for pair in range(half):
            out = dot(wy_ref[...], packed_ref[field, pair * rows : (pair + 1) * rows])
            out = out[:MODES] + out[MODES:]
            modes_ref[field, pair * MODES : (pair + 1) * MODES] = out[:, :LANES] + out[:, LANES:]

    for field in range(fields):
        for copy in loads[field]:
            copy.wait()
        sides = []
        for side in range(2):
            part = pl.ds(side * half, half)
            tile_of = [ext_ref[field, part, tile, main].reshape(half * rows, LANES) for tile in range(tiles)]
            diff = jnp.concatenate(tile_of, axis=1) - other_ref[field, part].reshape(half * rows, cols)
            high, low = split(diff)
            both = dot(high, weights) + dot(low, weights)
            sides.append(both + pltpu.roll(both, MODES, 1))
        high, low = split(jnp.where(lane < MODES, sides[0], sides[1]))
        packed_ref[field, :, :LANES] = high
        packed_ref[field, :, LANES:] = low
        if field:
            rows_of(field - 1)
    for copy in loads[fields]:
        copy.wait()
    rows_of(fields - 1)
    mine = facts[2]
    for piece in range(pieces):
        source = pl.multiple_of(jnp.bitwise_xor(mine, piece) * chunk, SUB)
        target = keep_ref if piece < pieces // 2 else send_ref
        target[piece % (pieces // 2)] = modes_ref[:, pl.ds(source, chunk)]

    upper = lax.broadcasted_iota(jnp.int32, (SUB, LANES), 0) >= 4

    def pack(bottom):
        for out_ref, last in ((a_ref, bottom), (b_ref, 1 - bottom)):
            here = pl.ds(GUARD + SUB + last * (rows - SUB), SUB)
            for level in range(levels):
                for tile in range(tiles):
                    lanes = pl.ds(tile * LANES, LANES)
                    u, v, w, p, t, s = (ext_ref[item, level, tile, here] for item in range(6))
                    out_ref[level, 0, :, lanes] = p
                    out_ref[level, 1, :, lanes] = v
                    for place, own, more in ((2, u, w), (3, t, s)):
                        more = pltpu.roll(more, 4, 0)
                        out_ref[level, place, :, lanes] = jnp.where(upper, own, more) if last else jnp.where(upper, more, own)

    for bottom in range(2):
        pl.when(facts[4] == bottom)(functools.partial(pack, bottom))


def nudge_kernel(facts, rate_ref, ext_ref, own_ref, far_ref, wide_ref, by_ref, out_ref, modes_ref, back_ref, done_ref, sem):
    fields, levels, rows, cols = out_ref.shape
    tiles = cols // LANES
    half = levels // 2
    pieces = 2 * own_ref.shape[0]
    chunk = own_ref.shape[2]
    mine = facts[2]
    for piece in range(pieces):
        target = pl.multiple_of(jnp.bitwise_xor(mine, piece) * chunk, SUB)
        source = own_ref if piece < pieces // 2 else far_ref
        modes_ref[:, pl.ds(target, chunk)] = source[piece % (pieces // 2)]
    lane = lax.broadcasted_iota(jnp.int32, (MODES, LANES), 1)
    lower = lax.broadcasted_iota(jnp.int32, (rows, LANES), 1) < MODES
    main = pl.ds(GUARD + SUB, rows)
    last_lane = lax.broadcasted_iota(jnp.int32, (rows, LANES), 1) == LANES - 1

    def back(field):
        for pair in range(half):
            factor = jnp.where(lane < MODES, rate_ref[field, pair], rate_ref[field, pair + half])
            high, low = split(modes_ref[field, pair * MODES : (pair + 1) * MODES] * factor)
            out = dot(by_ref[...], jnp.concatenate([high, low], axis=1))
            out = out[:rows] + out[rows:]
            out = out[:, :LANES] + out[:, LANES:]
            high, low = split(out)
            high_turned, low_turned = split(pltpu.roll(out, MODES, 1))
            here = pl.ds(pair * rows, rows)
            back_ref[field, 0, here, :LANES] = jnp.where(lower, high, low_turned)
            back_ref[field, 1, here, :LANES] = jnp.where(lower, high_turned, low)
            for side in range(2):
                back_ref[field, side, here, LANES:] = high

    for field in range(fields):
        back(field)
    stores = []
    for field in range(fields):
        for level in range(levels):
            if level % half == 0:
                side = level // half
                tendency = dot(back_ref[field, side], wide_ref[side])
            first = (level % half) * rows
            for tile in range(tiles):
                lanes = pl.ds(tile * LANES, LANES)
                value = ext_ref[field, level, tile, main]
                if field == 0:
                    before = ext_ref[field, level, (tile - 1) % (tiles + 1), main]
                    value = pltpu.roll(jnp.where(last_lane, before, value), 1, 1)
                done_ref[field, level, :, lanes] = value - tendency[first : first + rows, lanes.start : lanes.start + LANES]
            if level % half == half - 1:
                part = pl.ds(level + 1 - half, half)
                place = sem.at[field, level // half]
                stores.append(pltpu.make_async_copy(done_ref.at[field, part], out_ref.at[field, part], place))
                stores[-1].start()
    for copy in stores:
        copy.wait()


def band_lanes(level_count):
    starts = lane_starts(level_count)
    for item in range(6):
        for level in range(level_count):
            yield item, level, REACH_X[item], GROUP_X[item], starts[item] + REACH_X[item] * level


def pack_bands(facts, bands, ext_ref, parts, tiles):
    levels = ext_ref.shape[1]
    lane = lax.broadcasted_iota(jnp.int32, (SUB, LANES), 1)

    def pack(band, right):
        packed = [[jnp.zeros((SUB, LANES), jnp.float32) for _ in range(2)] for _ in parts]
        for item, level, width, group, first in band_lanes(levels):
            inside = (lane >= first) & (lane < first + width)
            for place, part in enumerate(parts):
                tile = ext_ref[item, level, (tiles - 1) * right, pl.ds(part * SUB + GUARD, SUB)]
                moved = pltpu.roll(tile, (first + right * width) % LANES, 1)
                packed[place][group] = jnp.where(inside, moved, packed[place][group])
        for place, part in enumerate(parts):
            for group in range(2):
                band[pl.ds(part * SUB, SUB), group * LANES : (group + 1) * LANES] = packed[place][group]

    for index, band in enumerate(bands):
        for right in range(2):
            pl.when((facts[3] ^ index) == right)(functools.partial(pack, band, right))


def shift_down(ext_ref, parts, tiles):
    lane = lax.broadcasted_iota(jnp.int32, (SUB, LANES), 1)
    for part in parts:
        here = pl.ds(part * SUB + GUARD, SUB)
        for level in range(ext_ref.shape[1]):
            old = [ext_ref[0, level, tile, here] for tile in range(tiles)]
            old += [old[0], old[0]]
            for tile in range(tiles + 1):
                value = old[tile] if tile >= tiles - 1 else jnp.where(lane == 0, old[tile + 1], old[tile])
                ext_ref[0, level, tile, here] = pltpu.roll(value, LANES - 1, 1)


def prepare_kernel(facts, _, bx_hbm, by_hbm, ext_ref, wide_ref, by_ref, *refs, rows, cols):
    *bands, sem = refs
    levels = ext_ref.shape[1]
    tiles = cols // LANES
    tables = [pltpu.make_async_copy(by_hbm.at[facts[1]], by_ref, sem.at[3, 0])]
    for side in range(2):
        for block, part in ((0, 0), (1, 0), (2 + side, 1)):
            target = wide_ref.at[side, pl.ds(block * MODES, MODES)]
            tables.append(pltpu.make_async_copy(bx_hbm.at[facts[0], part], target, sem.at[min(block, 2), side]))
    for copy in tables:
        copy.start()
    for side in range(2):
        wide_ref[side, (3 - side) * MODES : (4 - side) * MODES] = jnp.zeros((MODES, cols), wide_ref.dtype)
    zero = jnp.zeros((SUB, LANES), jnp.float32)
    for item in (1, 3):
        for level in range(levels):
            for tile in range(tiles + 1):
                ext_ref[item, level, tile, pl.ds(0, SUB)] = zero
                ext_ref[item, level, tile, pl.ds(GUARD + 2 * SUB + rows, SUB)] = zero
    parts = range(1, rows // SUB + 1)
    pack_bands(facts, bands, ext_ref, parts, tiles)
    shift_down(ext_ref, parts, tiles)
    for copy in tables:
        copy.wait()


def band_kernel(facts, *refs, x_phases, rows, cols):
    slabs = refs[1 + x_phases : 3 + x_phases]
    ext_ref, *bands = refs[3 + x_phases :]
    levels = ext_ref.shape[1]
    tiles = cols // LANES

    def place_slabs(odd):
        for phase, slab in enumerate(slabs):
            base = GUARD if (odd == 1) == (phase == 0) else GUARD + SUB + rows
            for item, place, turn in ((3, 0, 0), (1, 1, 0), (0, 2, 0), (2, 2, 4), (4, 3, 0), (5, 3, 4)):
                for level in range(levels):
                    for tile in range(tiles):
                        lanes = slice(tile * LANES, (tile + 1) * LANES)
                        value = slab[level, place, :, lanes]
                        if turn:
                            value = pltpu.roll(value, turn, 0)
                        ext_ref[item, level, tile, pl.ds(base, SUB)] = value

    for odd in range(2):
        pl.when(facts[6] == odd)(functools.partial(place_slabs, odd))
    parts = (0, rows // SUB + 1)
    pack_bands(facts, bands, ext_ref, parts, tiles)
    shift_down(ext_ref, parts, tiles)


def substep_kernel(facts, *refs, step, levels, rows, cols):
    bands, ext_ref = refs[1:-1], refs[-1]
    tiles = cols // LANES
    chunks = rows // SUB
    lane = lax.broadcasted_iota(jnp.int32, (SUB, LANES), 1)

    def unpack_bands(odd):
        for item, level, width, group, first in band_lanes(levels):
            down = 1 if item == 0 else 0
            for part in range(chunks + 2):
                here = pl.ds(part * SUB + GUARD, SUB)
                value = edge = jnp.zeros((SUB, LANES), jnp.float32)
                if down:
                    value = jnp.where(lane == LANES - 1, ext_ref[0, level, tiles, here], value)
                for phase, band in enumerate(bands):
                    left = odd if phase == 0 else 1 - odd
                    source = band[pl.ds(part * SUB, SUB), group * LANES : (group + 1) * LANES]
                    moved = pltpu.roll(source, (2 * LANES - first - left * width - down) % LANES, 1)
                    if left:
                        inside = (lane >= LANES - width - down) & (lane < LANES - down)
                    else:
                        inside = lane < width - down
                        edge = moved
                    value = jnp.where(inside, moved, value)
                ext_ref[item, level, tiles, here] = value
                if down:
                    old = ext_ref[0, level, tiles - 1, here]
                    ext_ref[0, level, tiles - 1, here] = jnp.where(lane == LANES - 1, edge, old)

    if step == 0:
        for odd in range(2):
            pl.when(facts[5] == odd)(functools.partial(unpack_bands, odd))

    quarter = 0.5 * COURANT
    sides = [jnp.where(facts[place] == 1, 1.0, 0.0) for place in (7, 8, 9, 10)]
    has_left, has_right, has_top, has_bottom = sides
    inner = jnp.where(lane == LANES - 1, has_right, 1.0)
    outer = jnp.where(lane < LANES // 2, has_right, jnp.where(lane == LANES - 1, 1.0, has_left))
    ring = tiles + 1

    def ahead(values, tile, count):
        moved = jnp.where(lane < count, values[(tile + 1) % ring], values[tile])
        return pltpu.roll(moved, LANES - count, 1)

    def behind(values, tile, count):
        moved = jnp.where(lane >= LANES - count, values[(tile - 1) % ring], values[tile])
        return pltpu.roll(moved, count, 1)

    u_ref, v_ref, w_ref, p_ref, t_ref, s_ref = (ext_ref.at[item] for item in range(6))
    first, last = step == 0, step == SUBSTEPS - 1

    def flush(pending):
        for ref, level, tile, here, value in pending:
            ref[level, tile, here] = value

    def winds(chunk, only_v=False):
        row = GUARD + chunk * SUB
        here = pl.ds(row, SUB)
        x_tiles = tiles if last else ring
        limit = {0: has_top, chunks + 1: has_bottom}.get(chunk)
        before = None
        line = None if only_v else [p_ref[0, tile, here] for tile in range(ring)]
        for level in range(levels):
            made = []
            for tile in range(x_tiles):
                slope = p_ref[level, tile, pl.ds(row + 1, SUB)] - p_ref[level, tile, pl.ds(row - 1, SUB)]
                if first:
                    slope = slope * (quarter if limit is None else quarter * limit)
                elif limit is not None:
                    slope = slope * limit
                made.append((v_ref, level, tile, here, v_ref[level, tile, here] - slope))
            if only_v:
                flush(made)
                continue
            old = [u_ref[level, tile, here] for tile in range(ring)]
            fresh = []
            for tile in range(ring):
                slope = ahead(line, tile, 2) - line[tile]
                edge = {tiles - 1: inner, tiles: outer}.get(tile)
                if first:
                    slope = slope * (quarter if edge is None else quarter * edge)
                elif edge is not None:
                    slope = slope * edge
                fresh.append(old[tile] - slope)
            for tile in range(ring):
                made.append((u_ref, level, tile, here, fresh[tile]))
            after = None
            if level + 1 < levels:
                after = [p_ref[level + 1, tile, here] for tile in range(ring)]
            for tile in range(x_tiles):
                if level == 0:
                    lift = after[tile]
                elif level == levels - 1:
                    lift = -before[tile]
                else:
                    lift = after[tile] - before[tile]
                warm = t_ref[level, tile, here]
                if first:
                    lift, warm = quarter * lift, COURANT * warm
                made.append((w_ref, level, tile, here, w_ref[level, tile, here] - (lift - warm)))
            before, line = line, after
            flush(made)

    def scalars(chunk):
        row = GUARD + chunk * SUB
        here = pl.ds(row, SUB)
        x_tiles = tiles if last else ring
        before, now = None, [w_ref[0, tile, here] for tile in range(x_tiles)]
        for level in range(levels):
            made = []
            line = [u_ref[level, tile, here] for tile in range(ring)]
            after = None
            if level + 1 < levels:
                after = [w_ref[level + 1, tile, here] for tile in range(x_tiles)]
            for tile in range(x_tiles):
                spread = line[tile] - behind(line, tile, 2)
                spread += v_ref[level, tile, pl.ds(row + 1, SUB)] - v_ref[level, tile, pl.ds(row - 1, SUB)]
                if level == 0:
                    spread += after[tile]
                elif level == levels - 1:
                    spread -= before[tile]
                else:
                    spread += after[tile] - before[tile]
                press, warm, speed = (ref[level, tile, here] for ref in (p_ref, t_ref, s_ref))
                if first:
                    press, warm, speed = quarter * press, COURANT * warm, (quarter * quarter) * speed
                    made.append((s_ref, level, tile, here, speed))
                press = press - speed * spread
                warm = warm - (COURANT * COURANT) * now[tile]
                if last:
                    press, warm = press * (1.0 / quarter), warm * (1.0 / COURANT)
                made.append((p_ref, level, tile, here, press))
                made.append((t_ref, level, tile, here, warm))
            before, now = now, after
            flush(made)

    if last:
        winds(0, True)
        winds(chunks + 1, True)
    span = range(1, chunks + 1) if last else range(chunks + 2)
    for chunk in span:
        winds(chunk)
    for chunk in span:
        scalars(chunk)


def solution(mesh):
    nx, ny = mesh.shape["gx"], mesh.shape["gy"]
    devices = nx * ny
    stages, middle = stages_of(devices)
    pieces = 1
    for stage in stages:
        pieces *= 1 << len(stage)
    pieces = max(pieces, 2)

    def decode(ref):
        number = ref[0]
        gx, gy = lax.div(number, ny), lax.rem(number, ny)
        mine = 0
        for stage in stages:
            for bit in reversed(stage):
                mine = mine * 2 + ((number >> bit) & 1)
        return (
            gx,
            gy,
            mine,
            (gx + 1) % 2,
            (gy + 1) % 2,
            gx % 2,
            gy % 2,
            jnp.where(gx > 0, 1, 0),
            jnp.where(gx < nx - 1, 1, 0),
            jnp.where(gy > 0, 1, 0),
            jnp.where(gy < ny - 1, 1, 0),
        )

    def informed(kernel, **static):
        def body(info, *refs):
            return kernel(decode(info), *refs, **static)

        return body

    x_phases = 1 if nx == 2 else 2

    def swap(value, mask):
        return lax.ppermute(value, ("gx", "gy"), [(i, i ^ mask) for i in range(devices)])

    def neighbours(value, axis, count, phase):
        pairs = []
        for low in range(phase, count - 1, 2):
            pairs += [(low, low + 1), (low + 1, low)]
        return lax.ppermute(value, axis, pairs)

    def on_device(state, driving, rate, sound_square):
        fields, levels, rows, cols = state.shape
        half = levels // 2
        chunk = half * MODES // pieces
        info = (lax.axis_index("gx") * ny + lax.axis_index("gy")).reshape(1)

        basis_x, weight_x = bases(MODES, cols * nx)
        basis_y, weight_y = bases(MODES, rows * ny)
        high, low = halves(weight_x)
        wx = np.concatenate([high, low], axis=0).T.reshape(nx, cols, 2 * MODES)
        high, low = halves(weight_y)
        wy = np.concatenate([high, low], axis=0).reshape(2 * MODES, ny, rows).transpose(1, 0, 2)
        high, low = halves(basis_x)
        bx = np.stack([high, low]).reshape(2, MODES, nx, cols).transpose(2, 0, 1, 3)
        high, low = halves(basis_y)
        by = np.stack([high, low]).reshape(2, MODES, ny, rows).transpose(2, 0, 3, 1).reshape(ny, 2 * rows, MODES)
        wx, wy, bx, by = (jnp.asarray(np.ascontiguousarray(t)) for t in (wx, wy, bx, by))

        hbm = pl.BlockSpec(memory_space=pltpu.HBM)
        vmem = pl.BlockSpec(memory_space=pltpu.VMEM)

        def call(kernel, name, shapes, ins, scratch, operands, flops=0, data=0, prefetch=1, aliases=None, limit=VMEM_LIMIT):
            return pl.pallas_call(
                kernel,
                grid_spec=pltpu.PrefetchScalarGridSpec(
                    num_scalar_prefetch=prefetch,
                    grid=(),
                    in_specs=ins,
                    out_specs=[vmem if name != "nudge" else hbm for _ in shapes],
                    scratch_shapes=scratch,
                ),
                out_shape=shapes,
                input_output_aliases=aliases or {},
                compiler_params=pltpu.CompilerParams(vmem_limit_bytes=limit),
                cost_estimate=pl.CostEstimate(flops=flops, bytes_accessed=data, transcendentals=0),
            )(*operands)

        def array(shape, dtype=jnp.float32):
            return jax.ShapeDtypeStruct(shape, dtype)

        tiles = cols // LANES
        slab_shape = (levels, 4, SUB, cols)
        piece_shape = (pieces // 2, fields, chunk, LANES)
        ext_shape = (6, levels, tiles + 1, rows + 2 * SUB + 2 * GUARD, LANES)
        band_shape = (rows + 2 * SUB, 2 * LANES)
        ext, slab_a, slab_b, keep, send = call(
            informed(head_kernel),
            "head",
            [array(ext_shape), *[array(slab_shape)] * 2, *[array(piece_shape)] * 2],
            [hbm] * 5,
            [
                pltpu.VMEM((fields, levels, rows, cols), jnp.float32),
                pltpu.VMEM((cols, 2 * MODES), jnp.bfloat16),
                pltpu.VMEM((2 * MODES, rows), jnp.bfloat16),
                pltpu.VMEM((fields, half * rows, 2 * LANES), jnp.bfloat16),
                pltpu.VMEM((fields, half * MODES, LANES), jnp.float32),
                pltpu.SemaphoreType.DMA((fields + 2, tiles + 1)),
            ],
            (info, *(pltpu.with_memory_space_constraint(x, pltpu.HBM) for x in (state, driving, sound_square, wx, wy))),
            600_000_000,
            9_000_000,
        )
        slab_a = neighbours(slab_a, "gy", ny, 0)
        slab_b = neighbours(slab_b, "gy", ny, 1)

        ext, wide, back, *bands = call(
            informed(prepare_kernel, rows=rows, cols=cols),
            "prepare",
            [array(ext_shape), array((2, 4 * MODES, cols), jnp.bfloat16), array((2 * rows, MODES), jnp.bfloat16)]
            + [array(band_shape)] * x_phases,
            [vmem, hbm, hbm],
            [pltpu.SemaphoreType.DMA((4, 2))],
            (info, ext, bx, by),
            1_000_000,
            5_000_000,
            aliases={1: 0},
        )
        ext, *bands = call(
            informed(band_kernel, x_phases=x_phases, rows=rows, cols=cols),
            "band",
            [array(ext_shape)] + [array(band_shape)] * x_phases,
            [vmem] * (3 + x_phases),
            [],
            (info, ext, *bands, slab_a, slab_b),
            1_000_000,
            5_000_000,
            aliases={1 + index: index for index in range(1 + x_phases)},
        )
        bands = [neighbours(band, "gx", nx, index) for index, band in enumerate(bands)]

        for step in range(SUBSTEPS):
            extra = bands if step == 0 else []
            (ext,) = call(
                informed(substep_kernel, step=step, levels=levels, rows=rows, cols=cols),
                f"substep_{step}",
                [array(ext_shape)],
                [vmem] * (1 + len(extra)),
                [],
                (info, ext, *extra),
                10_000_000,
                8_000_000,
                aliases={1: 0},
            )

        value = None
        for place, stage in enumerate(stages):
            masks = masks_of(stage)
            if place == 0:
                value = keep + swap(send, masks[1])
                continue
            value = value.reshape((len(masks), value.shape[0] // len(masks)) + value.shape[1:])
            moved = [swap(value[i], masks[i]) for i in range(1, len(masks))]
            value = functools.reduce(jnp.add, moved, value[0])
        moved = [swap(value, mask) for i, mask in enumerate(masks_of(middle)) if i]
        value = functools.reduce(jnp.add, moved, value)
        for place in reversed(range(1, len(stages))):
            moved = [swap(value, mask) for i, mask in enumerate(masks_of(stages[place])) if i]
            value = jnp.concatenate([value] + moved, axis=0)
        far = swap(value, masks_of(stages[0])[1])

        (out,) = call(
            informed(nudge_kernel),
            "nudge",
            [array(state.shape)],
            [vmem] * 5,
            [
                pltpu.VMEM((fields, half * MODES, LANES), jnp.float32),
                pltpu.VMEM((fields, 2, half * rows, 2 * LANES), jnp.bfloat16),
                pltpu.VMEM((fields, levels, rows, cols), jnp.float32),
                pltpu.SemaphoreType.DMA((fields, 2)),
            ],
            (info, rate, ext, value, far, wide, back),
            600_000_000,
            8_500_000,
            prefetch=2,
        )
        return out

    return jax.shard_map(
        on_device,
        mesh=mesh,
        in_specs=(P(None, None, "gy", "gx"), P(None, None, "gy", "gx"), P(), P(None, "gy", "gx")),
        out_specs=P(None, None, "gy", "gx"),
        check_vma=False,
    )
```

```python
import functools

import jax
import jax.numpy as jnp
import numpy as np
from jax import lax
from jax.experimental import pallas as pl
from jax.experimental.pallas import tpu as pltpu
from jax.sharding import PartitionSpec as P


MODES = 64
SUBSTEPS = 3
COURANT = 0.5
LANES = 128
SUB = 8
GUARD = 8
VMEM_LIMIT = 32 << 20

REACH_X = (5, 4, 4, 6, 4, 4)
GROUP_X = (0, 0, 1, 0, 1, 1)


def lane_starts(levels):
    used = [0, 0]
    starts = []
    for width, group in zip(REACH_X, GROUP_X):
        starts.append(used[group])
        used[group] += width * levels
    assert max(used) <= LANES
    return starts


def bases(count, total):
    index = np.arange(total, dtype=np.int64)
    order = np.arange(count, dtype=np.int64)
    freq = np.where(order < count // 2, order, order - count // 2 + 1)
    wrapped = (freq[:, None] * (2 * index[None, :] + 1)) % (2 * total)
    phase = np.pi * wrapped.astype(np.float64) / total
    basis = np.where(order[:, None] < count // 2, np.cos(phase), np.sin(phase))
    scaling = np.where(order == 0, 1.0 / total, 2.0 / total)
    basis32 = basis.astype(np.float32)
    weight32 = (basis * scaling[:, None]).astype(np.float32)
    return basis32, weight32


def halves(table):
    high = table.astype(jnp.bfloat16)
    low = (table - high.astype(np.float32)).astype(jnp.bfloat16)
    return np.asarray(high), np.asarray(low)


def split(value):
    high = value.astype(jnp.bfloat16)
    low = (value - high.astype(jnp.float32)).astype(jnp.bfloat16)
    return high, low


def dot(left, right):
    return jnp.dot(left, right, preferred_element_type=jnp.float32)


def masks_of(bits):
    masks = [0]
    for bit in bits:
        masks = masks + [mask | (1 << bit) for mask in masks]
    return masks


def stages_of(devices):
    total = devices.bit_length() - 1
    assert devices == 1 << total
    left = list(range(total))
    stages = []
    if left:
        stages.append([left.pop(0)])
    while len(left) > 3 and len(stages) < 3:
        stages.append([left.pop(0), left.pop()])
    return stages, left


def head_kernel(
    facts,
    state_ref,
    driving_ref,
    sound_ref,
    wx_hbm,
    wy_hbm,
    ext_ref,
    a_ref,
    b_ref,
    keep_ref,
    send_ref,
    other_ref,
    wx_ref,
    wy_ref,
    packed_ref,
    modes_ref,
    sem,
):
    fields, levels, rows, cols = state_ref.shape
    tiles = cols // LANES
    half = levels // 2
    pieces = 2 * keep_ref.shape[0]
    chunk = keep_ref.shape[2]
    main = pl.ds(GUARD + SUB, rows)

    def fetch(item):
        source = state_ref.at[item] if item < fields else sound_ref
        copies = [
            pltpu.make_async_copy(
                source.at[:, :, pl.ds(tile * LANES, LANES)], ext_ref.at[item, :, tile, main], sem.at[item, tile]
            )
            for tile in range(tiles)
        ]
        if item < fields:
            copies.append(pltpu.make_async_copy(driving_ref.at[item], other_ref.at[item], sem.at[item, tiles]))
        return copies

    tables = [
        pltpu.make_async_copy(wx_hbm.at[facts[0]], wx_ref, sem.at[fields + 1, 0]),
        pltpu.make_async_copy(wy_hbm.at[facts[1]], wy_ref, sem.at[fields + 1, 1]),
    ]
    loads = [fetch(item) for item in range(fields + 1)]
    for copy in [*tables, *(copy for load in loads for copy in load)]:
        copy.start()
    lane = lax.broadcasted_iota(jnp.int32, (half * rows, LANES), 1)
    for copy in tables:
        copy.wait()
    weights = wx_ref[...]

    def rows_of(field):
        for pair in range(half):
            out = dot(wy_ref[...], packed_ref[field, pair * rows : (pair + 1) * rows])
            out = out[:MODES] + out[MODES:]
            modes_ref[field, pair * MODES : (pair + 1) * MODES] = out[:, :LANES] + out[:, LANES:]

    for field in range(fields):
        for copy in loads[field]:
            copy.wait()
        sides = []
        for side in range(2):
            part = pl.ds(side * half, half)
            tile_of = [ext_ref[field, part, tile, main].reshape(half * rows, LANES) for tile in range(tiles)]
            diff = jnp.concatenate(tile_of, axis=1) - other_ref[field, part].reshape(half * rows, cols)
            high, low = split(diff)
            both = dot(high, weights) + dot(low, weights)
            sides.append(both + pltpu.roll(both, MODES, 1))
        high, low = split(jnp.where(lane < MODES, sides[0], sides[1]))
        packed_ref[field, :, :LANES] = high
        packed_ref[field, :, LANES:] = low
        if field:
            rows_of(field - 1)
    for copy in loads[fields]:
        copy.wait()
    rows_of(fields - 1)
    mine = facts[2]
    for piece in range(pieces):
        source = pl.multiple_of(jnp.bitwise_xor(mine, piece) * chunk, SUB)
        target = keep_ref if piece < pieces // 2 else send_ref
        target[piece % (pieces // 2)] = modes_ref[:, pl.ds(source, chunk)]

    upper = lax.broadcasted_iota(jnp.int32, (SUB, LANES), 0) >= 4

    def pack(bottom):
        for out_ref, last in ((a_ref, bottom), (b_ref, 1 - bottom)):
            here = pl.ds(GUARD + SUB + last * (rows - SUB), SUB)
            for level in range(levels):
                for tile in range(tiles):
                    lanes = pl.ds(tile * LANES, LANES)
                    u, v, w, p, t, s = (ext_ref[item, level, tile, here] for item in range(6))
                    out_ref[level, 0, :, lanes] = p
                    out_ref[level, 1, :, lanes] = v
                    for place, own, more in ((2, u, w), (3, t, s)):
                        more = pltpu.roll(more, 4, 0)
                        out_ref[level, place, :, lanes] = jnp.where(upper, own, more) if last else jnp.where(upper, more, own)

    for bottom in range(2):
        pl.when(facts[4] == bottom)(functools.partial(pack, bottom))


def nudge_kernel(facts, rate_ref, ext_ref, own_ref, far_ref, wide_ref, by_ref, out_ref, modes_ref, back_ref, done_ref, sem):
    fields, levels, rows, cols = out_ref.shape
    tiles = cols // LANES
    half = levels // 2
    pieces = 2 * own_ref.shape[0]
    chunk = own_ref.shape[2]
    mine = facts[2]
    for piece in range(pieces):
        target = pl.multiple_of(jnp.bitwise_xor(mine, piece) * chunk, SUB)
        source = own_ref if piece < pieces // 2 else far_ref
        modes_ref[:, pl.ds(target, chunk)] = source[piece % (pieces // 2)]
    lane = lax.broadcasted_iota(jnp.int32, (MODES, LANES), 1)
    lower = lax.broadcasted_iota(jnp.int32, (rows, LANES), 1) < MODES
    main = pl.ds(GUARD + SUB, rows)
    last_lane = lax.broadcasted_iota(jnp.int32, (rows, LANES), 1) == LANES - 1

    def back(field):
        for pair in range(half):
            factor = jnp.where(lane < MODES, rate_ref[field, pair], rate_ref[field, pair + half])
            high, low = split(modes_ref[field, pair * MODES : (pair + 1) * MODES] * factor)
            out = dot(by_ref[...], jnp.concatenate([high, low], axis=1))
            out = out[:rows] + out[rows:]
            out = out[:, :LANES] + out[:, LANES:]
            high, low = split(out)
            high_turned, low_turned = split(pltpu.roll(out, MODES, 1))
            here = pl.ds(pair * rows, rows)
            back_ref[field, 0, here, :LANES] = jnp.where(lower, high, low_turned)
            back_ref[field, 1, here, :LANES] = jnp.where(lower, high_turned, low)
            for side in range(2):
                back_ref[field, side, here, LANES:] = high

    for field in range(fields):
        back(field)
    stores = []
    for field in range(fields):
        for level in range(levels):
            if level % half == 0:
                side = level // half
                tendency = dot(back_ref[field, side], wide_ref[side])
            first = (level % half) * rows
            for tile in range(tiles):
                lanes = pl.ds(tile * LANES, LANES)
                value = ext_ref[field, level, tile, main]
                if field == 0:
                    before = ext_ref[field, level, (tile - 1) % (tiles + 1), main]
                    value = pltpu.roll(jnp.where(last_lane, before, value), 1, 1)
                done_ref[field, level, :, lanes] = value - tendency[first : first + rows, lanes.start : lanes.start + LANES]
            if level % half == half - 1:
                part = pl.ds(level + 1 - half, half)
                place = sem.at[field, level // half]
                stores.append(pltpu.make_async_copy(done_ref.at[field, part], out_ref.at[field, part], place))
                stores[-1].start()
    for copy in stores:
        copy.wait()


def band_lanes(level_count):
    starts = lane_starts(level_count)
    for item in range(6):
        for level in range(level_count):
            yield item, level, REACH_X[item], GROUP_X[item], starts[item] + REACH_X[item] * level


def pack_bands(facts, bands, ext_ref, parts, tiles):
    levels = ext_ref.shape[1]
    lane = lax.broadcasted_iota(jnp.int32, (SUB, LANES), 1)

    def pack(band, right):
        packed = [[jnp.zeros((SUB, LANES), jnp.float32) for _ in range(2)] for _ in parts]
        for item, level, width, group, first in band_lanes(levels):
            inside = (lane >= first) & (lane < first + width)
            for place, part in enumerate(parts):
                tile = ext_ref[item, level, (tiles - 1) * right, pl.ds(part * SUB + GUARD, SUB)]
                moved = pltpu.roll(tile, (first + right * width) % LANES, 1)
                packed[place][group] = jnp.where(inside, moved, packed[place][group])
        for place, part in enumerate(parts):
            for group in range(2):
                band[pl.ds(part * SUB, SUB), group * LANES : (group + 1) * LANES] = packed[place][group]

    for index, band in enumerate(bands):
        for right in range(2):
            pl.when((facts[3] ^ index) == right)(functools.partial(pack, band, right))


def shift_down(ext_ref, parts, tiles):
    lane = lax.broadcasted_iota(jnp.int32, (SUB, LANES), 1)
    for part in parts:
        here = pl.ds(part * SUB + GUARD, SUB)
        for level in range(ext_ref.shape[1]):
            old = [ext_ref[0, level, tile, here] for tile in range(tiles)]
            old += [old[0], old[0]]
            for tile in range(tiles + 1):
                value = old[tile] if tile >= tiles - 1 else jnp.where(lane == 0, old[tile + 1], old[tile])
                ext_ref[0, level, tile, here] = pltpu.roll(value, LANES - 1, 1)


def prepare_kernel(facts, _, bx_hbm, by_hbm, ext_ref, wide_ref, by_ref, *refs, rows, cols):
    *bands, sem = refs
    levels = ext_ref.shape[1]
    tiles = cols // LANES
    tables = [pltpu.make_async_copy(by_hbm.at[facts[1]], by_ref, sem.at[3, 0])]
    for side in range(2):
        for block, part in ((0, 0), (1, 0), (2 + side, 1)):
            target = wide_ref.at[side, pl.ds(block * MODES, MODES)]
            tables.append(pltpu.make_async_copy(bx_hbm.at[facts[0], part], target, sem.at[min(block, 2), side]))
    for copy in tables:
        copy.start()
    for side in range(2):
        wide_ref[side, (3 - side) * MODES : (4 - side) * MODES] = jnp.zeros((MODES, cols), wide_ref.dtype)
    zero = jnp.zeros((SUB, LANES), jnp.float32)
    for item in (1, 3):
        for level in range(levels):
            for tile in range(tiles + 1):
                ext_ref[item, level, tile, pl.ds(0, SUB)] = zero
                ext_ref[item, level, tile, pl.ds(GUARD + 2 * SUB + rows, SUB)] = zero
    parts = range(1, rows // SUB + 1)
    pack_bands(facts, bands, ext_ref, parts, tiles)
    shift_down(ext_ref, parts, tiles)
    for copy in tables:
        copy.wait()


def band_kernel(facts, *refs, x_phases, rows, cols):
    slabs = refs[1 + x_phases : 3 + x_phases]
    ext_ref, *bands = refs[3 + x_phases :]
    levels = ext_ref.shape[1]
    tiles = cols // LANES

    def place_slabs(odd):
        for phase, slab in enumerate(slabs):
            base = GUARD if (odd == 1) == (phase == 0) else GUARD + SUB + rows
            for item, place, turn in ((3, 0, 0), (1, 1, 0), (0, 2, 0), (2, 2, 4), (4, 3, 0), (5, 3, 4)):
                for level in range(levels):
                    for tile in range(tiles):
                        lanes = slice(tile * LANES, (tile + 1) * LANES)
                        value = slab[level, place, :, lanes]
                        if turn:
                            value = pltpu.roll(value, turn, 0)
                        ext_ref[item, level, tile, pl.ds(base, SUB)] = value

    for odd in range(2):
        pl.when(facts[6] == odd)(functools.partial(place_slabs, odd))
    parts = (0, rows // SUB + 1)
    pack_bands(facts, bands, ext_ref, parts, tiles)
    shift_down(ext_ref, parts, tiles)


def substep_kernel(facts, *refs, step, levels, rows, cols, early=None):
    bands, ext_ref = refs[1:-1], refs[-1]
    tiles = cols // LANES
    chunks = rows // SUB
    lane = lax.broadcasted_iota(jnp.int32, (SUB, LANES), 1)

    def unpack_bands(odd):
        for item, level, width, group, first in band_lanes(levels):
            down = 1 if item == 0 else 0
            for part in range(chunks + 2):
                here = pl.ds(part * SUB + GUARD, SUB)
                value = edge = jnp.zeros((SUB, LANES), jnp.float32)
                if down:
                    value = jnp.where(lane == LANES - 1, ext_ref[0, level, tiles, here], value)
                for phase, band in enumerate(bands):
                    left = odd if phase == 0 else 1 - odd
                    source = band[pl.ds(part * SUB, SUB), group * LANES : (group + 1) * LANES]
                    moved = pltpu.roll(source, (2 * LANES - first - left * width - down) % LANES, 1)
                    if left:
                        inside = (lane >= LANES - width - down) & (lane < LANES - down)
                    else:
                        inside = lane < width - down
                        edge = moved
                    value = jnp.where(inside, moved, value)
                ext_ref[item, level, tiles, here] = value
                if down:
                    old = ext_ref[0, level, tiles - 1, here]
                    ext_ref[0, level, tiles - 1, here] = jnp.where(lane == LANES - 1, edge, old)

    if step == 0 and not early:
        for odd in range(2):
            pl.when(facts[5] == odd)(functools.partial(unpack_bands, odd))

    quarter = 0.5 * COURANT
    sides = [jnp.where(facts[place] == 1, 1.0, 0.0) for place in (7, 8, 9, 10)]
    has_left, has_right, has_top, has_bottom = sides
    inner = jnp.where(lane == LANES - 1, has_right, 1.0)
    outer = jnp.where(lane < LANES // 2, has_right, jnp.where(lane == LANES - 1, 1.0, has_left))
    ring = tiles + 1

    def ahead(values, tile, count):
        moved = jnp.where(lane < count, values[(tile + 1) % ring], values[tile])
        return pltpu.roll(moved, LANES - count, 1)

    def behind(values, tile, count):
        moved = jnp.where(lane >= LANES - count, values[(tile - 1) % ring], values[tile])
        return pltpu.roll(moved, count, 1)

    u_ref, v_ref, w_ref, p_ref, t_ref, s_ref = (ext_ref.at[item] for item in range(6))
    first, last = step == 0, step == SUBSTEPS - 1

    def flush(pending):
        for ref, level, tile, here, value in pending:
            ref[level, tile, here] = value

    def wanted(kind, chunk, tile):
        if early is None:
            return True
        low, high, count = {"u": (1, chunks, tiles - 1), "v": (2, chunks - 1, tiles), "w": (1, chunks, tiles)}[kind]
        return (low <= chunk <= high and tile < count) == early

    def winds(chunk, only_v=False):
        row = GUARD + chunk * SUB
        here = pl.ds(row, SUB)
        x_tiles = tiles if last else ring
        limit = {0: has_top, chunks + 1: has_bottom}.get(chunk)
        before = None
        line = None if only_v else [p_ref[0, tile, here] for tile in range(ring)]
        for level in range(levels):
            made = []
            for tile in range(x_tiles):
                if not wanted("v", chunk, tile):
                    continue
                slope = p_ref[level, tile, pl.ds(row + 1, SUB)] - p_ref[level, tile, pl.ds(row - 1, SUB)]
                if first:
                    slope = slope * (quarter if limit is None else quarter * limit)
                elif limit is not None:
                    slope = slope * limit
                made.append((v_ref, level, tile, here, v_ref[level, tile, here] - slope))
            if only_v:
                flush(made)
                continue
            for tile in range(ring):
                if not wanted("u", chunk, tile):
                    continue
                slope = ahead(line, tile, 2) - line[tile]
                edge = {tiles - 1: inner, tiles: outer}.get(tile)
                if first:
                    slope = slope * (quarter if edge is None else quarter * edge)
                elif edge is not None:
                    slope = slope * edge
                made.append((u_ref, level, tile, here, u_ref[level, tile, here] - slope))
            after = None
            if level + 1 < levels:
                after = [p_ref[level + 1, tile, here] for tile in range(ring)]
            for tile in range(x_tiles):
                if not wanted("w", chunk, tile):
                    continue
                if level == 0:
                    lift = after[tile]
                elif level == levels - 1:
                    lift = -before[tile]
                else:
                    lift = after[tile] - before[tile]
                warm = t_ref[level, tile, here]
                if first:
                    lift, warm = quarter * lift, COURANT * warm
                made.append((w_ref, level, tile, here, w_ref[level, tile, here] - (lift - warm)))
            before, line = line, after
            flush(made)

    def scalars(chunk):
        row = GUARD + chunk * SUB
        here = pl.ds(row, SUB)
        x_tiles = tiles if last else ring
        before, now = None, [w_ref[0, tile, here] for tile in range(x_tiles)]
        for level in range(levels):
            made = []
            line = [u_ref[level, tile, here] for tile in range(ring)]
            after = None
            if level + 1 < levels:
                after = [w_ref[level + 1, tile, here] for tile in range(x_tiles)]
            for tile in range(x_tiles):
                spread = line[tile] - behind(line, tile, 2)
                spread += v_ref[level, tile, pl.ds(row + 1, SUB)] - v_ref[level, tile, pl.ds(row - 1, SUB)]
                if level == 0:
                    spread += after[tile]
                elif level == levels - 1:
                    spread -= before[tile]
                else:
                    spread += after[tile] - before[tile]
                press, warm, speed = (ref[level, tile, here] for ref in (p_ref, t_ref, s_ref))
                if first:
                    press, warm, speed = quarter * press, COURANT * warm, (quarter * quarter) * speed
                    made.append((s_ref, level, tile, here, speed))
                press = press - speed * spread
                warm = warm - (COURANT * COURANT) * now[tile]
                if last:
                    press, warm = press * (1.0 / quarter), warm * (1.0 / COURANT)
                made.append((p_ref, level, tile, here, press))
                made.append((t_ref, level, tile, here, warm))
            before, now = now, after
            flush(made)

    if last:
        winds(0, True)
        winds(chunks + 1, True)
    span = range(1, chunks + 1) if last or early else range(chunks + 2)
    for chunk in span:
        winds(chunk)
    if not early:
        for chunk in span:
            scalars(chunk)


def solution(mesh):
    nx, ny = mesh.shape["gx"], mesh.shape["gy"]
    devices = nx * ny
    stages, middle = stages_of(devices)
    pieces = 1
    for stage in stages:
        pieces *= 1 << len(stage)
    pieces = max(pieces, 2)

    def decode(ref):
        number = ref[0]
        gx, gy = lax.div(number, ny), lax.rem(number, ny)
        mine = 0
        for stage in stages:
            for bit in reversed(stage):
                mine = mine * 2 + ((number >> bit) & 1)
        return (
            gx,
            gy,
            mine,
            (gx + 1) % 2,
            (gy + 1) % 2,
            gx % 2,
            gy % 2,
            jnp.where(gx > 0, 1, 0),
            jnp.where(gx < nx - 1, 1, 0),
            jnp.where(gy > 0, 1, 0),
            jnp.where(gy < ny - 1, 1, 0),
        )

    def informed(kernel, **static):
        def body(info, *refs):
            return kernel(decode(info), *refs, **static)

        return body

    x_phases = 1 if nx == 2 else 2

    def swap(value, mask):
        return lax.ppermute(value, ("gx", "gy"), [(i, i ^ mask) for i in range(devices)])

    def neighbours(value, axis, count, phase):
        pairs = []
        for low in range(phase, count - 1, 2):
            pairs += [(low, low + 1), (low + 1, low)]
        return lax.ppermute(value, axis, pairs)

    def on_device(state, driving, rate, sound_square):
        fields, levels, rows, cols = state.shape
        half = levels // 2
        chunk = half * MODES // pieces
        info = (lax.axis_index("gx") * ny + lax.axis_index("gy")).reshape(1)

        basis_x, weight_x = bases(MODES, cols * nx)
        basis_y, weight_y = bases(MODES, rows * ny)
        high, low = halves(weight_x)
        wx = np.concatenate([high, low], axis=0).T.reshape(nx, cols, 2 * MODES)
        high, low = halves(weight_y)
        wy = np.concatenate([high, low], axis=0).reshape(2 * MODES, ny, rows).transpose(1, 0, 2)
        high, low = halves(basis_x)
        bx = np.stack([high, low]).reshape(2, MODES, nx, cols).transpose(2, 0, 1, 3)
        high, low = halves(basis_y)
        by = np.stack([high, low]).reshape(2, MODES, ny, rows).transpose(2, 0, 3, 1).reshape(ny, 2 * rows, MODES)
        wx, wy, bx, by = (jnp.asarray(np.ascontiguousarray(t)) for t in (wx, wy, bx, by))

        hbm = pl.BlockSpec(memory_space=pltpu.HBM)
        vmem = pl.BlockSpec(memory_space=pltpu.VMEM)

        def call(kernel, name, shapes, ins, scratch, operands, flops=0, data=0, prefetch=1, aliases=None, limit=VMEM_LIMIT):
            return pl.pallas_call(
                kernel,
                grid_spec=pltpu.PrefetchScalarGridSpec(
                    num_scalar_prefetch=prefetch,
                    grid=(),
                    in_specs=ins,
                    out_specs=[vmem if name != "nudge" else hbm for _ in shapes],
                    scratch_shapes=scratch,
                ),
                out_shape=shapes,
                input_output_aliases=aliases or {},
                compiler_params=pltpu.CompilerParams(vmem_limit_bytes=limit),
                cost_estimate=pl.CostEstimate(flops=flops, bytes_accessed=data, transcendentals=0),
            )(*operands)

        def array(shape, dtype=jnp.float32):
            return jax.ShapeDtypeStruct(shape, dtype)

        tiles = cols // LANES
        slab_shape = (levels, 4, SUB, cols)
        piece_shape = (pieces // 2, fields, chunk, LANES)
        ext_shape = (6, levels, tiles + 1, rows + 2 * SUB + 2 * GUARD, LANES)
        band_shape = (rows + 2 * SUB, 2 * LANES)
        ext, slab_a, slab_b, keep, send = call(
            informed(head_kernel),
            "head",
            [array(ext_shape), *[array(slab_shape)] * 2, *[array(piece_shape)] * 2],
            [hbm] * 5,
            [
                pltpu.VMEM((fields, levels, rows, cols), jnp.float32),
                pltpu.VMEM((cols, 2 * MODES), jnp.bfloat16),
                pltpu.VMEM((2 * MODES, rows), jnp.bfloat16),
                pltpu.VMEM((fields, half * rows, 2 * LANES), jnp.bfloat16),
                pltpu.VMEM((fields, half * MODES, LANES), jnp.float32),
                pltpu.SemaphoreType.DMA((fields + 2, tiles + 1)),
            ],
            (info, *(pltpu.with_memory_space_constraint(x, pltpu.HBM) for x in (state, driving, sound_square, wx, wy))),
            600_000_000,
            9_000_000,
        )
        slab_a = neighbours(slab_a, "gy", ny, 0)
        slab_b = neighbours(slab_b, "gy", ny, 1)

        ext, wide, back, *bands = call(
            informed(prepare_kernel, rows=rows, cols=cols),
            "prepare",
            [array(ext_shape), array((2, 4 * MODES, cols), jnp.bfloat16), array((2 * rows, MODES), jnp.bfloat16)]
            + [array(band_shape)] * x_phases,
            [vmem, hbm, hbm],
            [pltpu.SemaphoreType.DMA((4, 2))],
            (info, ext, bx, by),
            1_000_000,
            5_000_000,
            aliases={1: 0},
        )
        (ext,) = call(
            informed(substep_kernel, step=0, levels=levels, rows=rows, cols=cols, early=True),
            "early",
            [array(ext_shape)],
            [vmem],
            [],
            (info, ext),
            10_000_000,
            8_000_000,
            aliases={1: 0},
        )
        ext, *bands = call(
            informed(band_kernel, x_phases=x_phases, rows=rows, cols=cols),
            "band",
            [array(ext_shape)] + [array(band_shape)] * x_phases,
            [vmem] * (3 + x_phases),
            [],
            (info, ext, *bands, slab_a, slab_b),
            1_000_000,
            5_000_000,
            aliases={1 + index: index for index in range(1 + x_phases)},
        )
        bands = [neighbours(band, "gx", nx, index) for index, band in enumerate(bands)]

        for step in range(SUBSTEPS):
            extra = bands if step == 0 else []
            (ext,) = call(
                informed(
                    substep_kernel, step=step, levels=levels, rows=rows, cols=cols, early=None if step else False
                ),
                f"substep_{step}",
                [array(ext_shape)],
                [vmem] * (1 + len(extra)),
                [],
                (info, ext, *extra),
                10_000_000,
                8_000_000,
                aliases={1: 0},
            )

        value = None
        for place, stage in enumerate(stages):
            masks = masks_of(stage)
            if place == 0:
                value = keep + swap(send, masks[1])
                continue
            value = value.reshape((len(masks), value.shape[0] // len(masks)) + value.shape[1:])
            moved = [swap(value[i], masks[i]) for i in range(1, len(masks))]
            value = functools.reduce(jnp.add, moved, value[0])
        moved = [swap(value, mask) for i, mask in enumerate(masks_of(middle)) if i]
        value = functools.reduce(jnp.add, moved, value)
        for place in reversed(range(1, len(stages))):
            moved = [swap(value, mask) for i, mask in enumerate(masks_of(stages[place])) if i]
            value = jnp.concatenate([value] + moved, axis=0)
        far = swap(value, masks_of(stages[0])[1])

        (out,) = call(
            informed(nudge_kernel),
            "nudge",
            [array(state.shape)],
            [vmem] * 5,
            [
                pltpu.VMEM((fields, half * MODES, LANES), jnp.float32),
                pltpu.VMEM((fields, 2, half * rows, 2 * LANES), jnp.bfloat16),
                pltpu.VMEM((fields, levels, rows, cols), jnp.float32),
                pltpu.SemaphoreType.DMA((fields, 2)),
            ],
            (info, rate, ext, value, far, wide, back),
            600_000_000,
            8_500_000,
            prefetch=2,
        )
        return out

    return jax.shard_map(
        on_device,
        mesh=mesh,
        in_specs=(P(None, None, "gy", "gx"), P(None, None, "gy", "gx"), P(), P(None, "gy", "gx")),
        out_specs=P(None, None, "gy", "gx"),
        check_vma=False,
    )
```
